32 devices in a mesh: dp: 8 (over y, x, core), tp: 4 (over z).
Axes of the slice: x: 2, y: 2, z: 4, core: 2. Of those that a mesh axis runs over, the one named last changes fastest.
Arguments:
- tokens: bfloat16 [8192, 1024], P(('dp', 'tp')), may hold values from -6 to 6
- cotangent: bfloat16 [8192, 1024], P(('dp', 'tp')), may hold values from -6 to 6
- seq_lengths: int32 [8, 2], P('dp'), may hold values from 0 to 1024, as said below
- attention_gain: float32 [1024], replicated, may hold values from 0.5 to 1.5
- query_weight: bfloat16 [1024, 1024], P(None, 'tp'), may hold values from -0.1875 to 0.1875
- latent_down: bfloat16 [1024, 512], replicated, may hold values from -0.1875 to 0.1875
- key_up: bfloat16 [256, 1024], P(None, 'tp'), may hold values from -0.375 to 0.375
- value_up: bfloat16 [256, 1024], P(None, 'tp'), may hold values from -0.375 to 0.375
- out_weight: bfloat16 [1024, 1024], P('tp'), may hold values from -1.5 to 1.5
- feedforward_gain: float32 [1024], replicated, may hold values from 0.5 to 1.5
- gate_weight: bfloat16 [1024, 2816], P(None, 'tp'), may hold values from -0.1875 to 0.1875
- up_weight: bfloat16 [1024, 2816], P(None, 'tp'), may hold values from -0.1875 to 0.1875
- down_weight: bfloat16 [2816, 1024], P('tp'), may hold values from -0.109375 to 0.109375
Outputs:
- output: bfloat16 [8192, 1024], P(('dp', 'tp'))
- tokens_grad: float32 [8192, 1024], P(('dp', 'tp'))
- attention_gain_grad: float32 [1024], P('dp')
- query_weight_grad: float32 [1024, 1024], P('dp', 'tp')
- latent_down_grad: float32 [1024, 512], P('dp', 'tp')
- key_up_grad: float32 [256, 1024], P('dp', 'tp')
- value_up_grad: float32 [256, 1024], P('dp', 'tp')
- out_weight_grad: float32 [1024, 1024], P('tp', 'dp')
- feedforward_gain_grad: float32 [1024], P('dp')
- gate_weight_grad: float32 [1024, 2816], P('dp', 'tp')
- up_weight_grad: float32 [1024, 2816], P('dp', 'tp')
- down_weight_grad: float32 [2816, 1024], P('tp', 'dp')
The draws below stay inside these ranges and needn't reach their ends.
Inputs may be any that keep to these rules, and one draw needn't show every extreme that they name: `seq_lengths`: row d gives the lengths of the two sequences packed, from row 0 on, into the 1024 tokens of index d of dp; they sum to 1024. Either one sequence fills the pack (second entry 0) or two sequences of half of 1024 each; both kinds occur in every draw.
All inputs are finite; a program needn't handle non-finite values.
Results may differ from the reference program's by a relative error of at most 0.014.
Values may be sent and summed in bfloat16 or wider, within the bound.
No kernel may reach another device: no remote copies, remote signals or barrier semaphores. Data moves between devices by JAX's collectives and lax.ppermute only.
A program may use at most 128 MiB of HBM per device.

```python
import jax
import jax.numpy as jnp
from jax import lax

D = 1024
HEADS = 16
HD = 64
LAT = 256
FF = 2816
TOK_DEV = 1024
TOKENS = 8192
N_DP = 8


def draw_seq_lengths(key, part):
    picked = jax.random.randint(key, (N_DP,), 0, 2)
    shuffled = jax.random.permutation(jax.random.fold_in(key, 11), N_DP)
    picked = picked.at[shuffled[0]].set(1)
    picked = picked.at[shuffled[1]].set(0)
    leading = jnp.where(picked == 1, TOK_DEV, TOK_DEV // 2)
    return jnp.stack([leading, TOK_DEV - leading], axis=1).astype(jnp.int32)


def spiked(entries, own_key, source, target, blocks, factor):
    def block_of(dim):
        return (jnp.arange(entries.shape[dim]) // (entries.shape[dim] // blocks)).reshape((-1,) + (1,) * (entries.ndim - 1 - dim))

    one_side = jax.random.permutation(own_key, blocks)[block_of(target)]
    other_side = (block_of(target) + blocks // 2) % blocks
    return jnp.where((block_of(source) == one_side) | (block_of(source) == other_side), factor * entries, entries)


def shard_levels(key, extent, split, low, high):
    loudness, own = 1.0, jax.random.fold_in(key, 6)
    for axis_at, parts in split:
        draws = jnp.exp(jax.random.uniform(jax.random.fold_in(own, axis_at), (parts,), jnp.float32, low / len(split), high / len(split)))
        loudness = loudness * jnp.repeat(draws, extent[axis_at] // parts).reshape([-1 if axis == axis_at else 1 for axis in range(len(extent))])
    return loudness


def scatter_about(key, shape, scale, limit, cuts=(), kind=jnp.bfloat16):
    array = jax.random.normal(key, shape, jnp.float32) * scale
    if len(cuts) > 0:
        array = shard_levels(key, shape, cuts, -0.22, 0.18) * array
    return jnp.clip(array, min=-limit, max=limit).astype(kind)


def noise_with(key, dims, spread, reach, shards, heavy, kind=jnp.bfloat16):
    drawn = spread * jax.random.normal(key, dims, jnp.float32)
    if shards:
        drawn = drawn * shard_levels(key, dims, shards, -0.22, 0.18)
    return jnp.clip(spiked(drawn, jax.random.fold_in(key, 3), *heavy), -reach, reach).astype(kind)


def setup_inputs(seed: int = 0) -> dict:
    seeds = jax.random.split(jax.random.key(seed), 14)
    return {
        "tokens": scatter_about(seeds[0], (TOKENS, D), 1.0, 6.0, ((0, 32),)),
        "cotangent": noise_with(seeds[1], (TOKENS, D), 1.0, 6.0, ((0, 32),), (0, 1, 32, 2.75)),
        "seq_lengths": draw_seq_lengths(jax.random.fold_in(seeds[13], 71), 0),
        "attention_gain": jnp.clip(1.0 + 0.1 * jax.random.normal(seeds[3], (D,), jnp.float32), 0.5, 1.5),
        "query_weight": scatter_about(seeds[4], (D, HEADS * HD), D ** -0.5, 0.1875, ((1, 4),)),
        "latent_down": scatter_about(seeds[5], (D, 2 * LAT), D ** -0.5, 0.1875),
        "key_up": scatter_about(seeds[6], (LAT, HEADS * HD), LAT ** -0.5, 0.375, ((1, 4),)),
        "value_up": scatter_about(seeds[7], (LAT, HEADS * HD), LAT ** -0.5, 0.375, ((1, 4),)),
        "out_weight": scatter_about(seeds[8], (HEADS * HD, D), (max(1, HEADS * HD * 16 // TOK_DEV)) ** -0.5, 1.5, ((0, 4),)),
        "feedforward_gain": jnp.clip(1.0 + 0.1 * jax.random.normal(seeds[9], (D,), jnp.float32), 0.5, 1.5),
        "gate_weight": scatter_about(seeds[10], (D, FF), D ** -0.5, 0.1875, ((1, 4),)),
        "up_weight": scatter_about(seeds[11], (D, FF), D ** -0.5, 0.1875, ((1, 4),)),
        "down_weight": scatter_about(seeds[12], (FF, D), FF ** -0.5, 0.109375, ((0, 4),)),
    }


norm_eps = 1e-06
masked_score = -1000000000.0
highest = lax.Precision.HIGHEST

@jax.custom_vjp
def low(v):
    return lax.optimization_barrier(v.astype(jnp.bfloat16)).astype(jnp.float32)

@jax.custom_vjp
def low_back(v):
    return v

def low_keep(v):
    return (low(v), None)

def low_pass(kept, grad):
    return (grad,)

def back_keep(v):
    return (v, None)

def back_low(kept, grad):
    return (low(grad),)
low.defvjp(low_keep, low_pass)
low_back.defvjp(back_keep, back_low)

def matmul(left, right):
    return jnp.dot(left, right, precision=highest, preferred_element_type=jnp.float32)

def rms_norm(values, scaling):
    factor = lax.rsqrt(lax.optimization_barrier(jnp.mean(values * values, axis=-1, keepdims=True)) + norm_eps)
    return values * factor * scaling

def visible_mask(start_row, block_rows, key_index, boundary):
    query_index = start_row + jnp.arange(block_rows, dtype=jnp.int32)
    same_doc = (key_index[None, :] >= boundary) == (query_index[:, None] >= boundary)
    return (key_index[None, :] <= query_index[:, None]) & same_doc

def attend(queries, keys_all, values_all, boundary):
    total_rows = queries.shape[0]
    block_rows = min(512, total_rows)
    blocks = total_rows // block_rows
    key_index = jnp.arange(total_rows, dtype=jnp.int32)
    factor = HD ** (-0.5)

    def block_fn(block_data):
        query_block, start_row = block_data
        allowed = visible_mask(start_row, block_rows, key_index, boundary)
        scores = low_back(jnp.einsum('qhd,khd->hqk', query_block, keys_all, precision=highest) * factor)
        scores = jnp.where(allowed[None], scores, masked_score)
        weights = low(jax.nn.softmax(scores, axis=-1))
        return jnp.einsum('hqk,khd->qhd', weights, values_all, precision=highest)
    checked = jax.checkpoint(block_fn)
    starts = jnp.arange(blocks, dtype=jnp.int32) * block_rows
    result = lax.map(checked, (queries.reshape(blocks, block_rows, HEADS, HD), starts))
    return result.reshape(total_rows, HEADS * HD)

def layer(params, inputs, boundary):
    attention_gain, query_weight, latent_down, key_up, value_up, out_weight, feedforward_gain, gate_weight, up_weight, down_weight = params
    total_rows = inputs.shape[0]
    normed_one = low(rms_norm(inputs, attention_gain))
    queries = low_back(low(matmul(normed_one, query_weight))).reshape(total_rows, HEADS, HD)
    latents = low_back(low(matmul(normed_one, latent_down))).reshape(total_rows, 2, LAT)
    key_parts = key_up.reshape(LAT, 2, HEADS // 2, HD)
    value_parts = value_up.reshape(LAT, 2, HEADS // 2, HD)
    keys_all = low_back(low(jnp.einsum('tgl,lgjd->tgjd', latents, key_parts, precision=highest))).reshape(total_rows, HEADS, HD)
    values_all = low_back(low(jnp.einsum('tgl,lgjd->tgjd', latents, value_parts, precision=highest))).reshape(total_rows, HEADS, HD)
    attended = low_back(low(attend(queries, keys_all, values_all, boundary)))
    mixed = inputs + low_back(matmul(attended, out_weight))
    normed_two = low(rms_norm(mixed, feedforward_gain))
    gate_rows = low_back(matmul(normed_two, gate_weight))
    up_rows = low_back(matmul(normed_two, up_weight))
    activated = low(jax.nn.silu(gate_rows) * up_rows)
    return mixed + low_back(matmul(activated, down_weight))

def reference(tokens, cotangent, seq_lengths, attention_gain, query_weight, latent_down, key_up, value_up, out_weight, feedforward_gain, gate_weight, up_weight, down_weight):
    params = tuple((weight.astype(jnp.float32) for weight in (attention_gain, query_weight, latent_down, key_up, value_up, out_weight, feedforward_gain, gate_weight, up_weight, down_weight)))
    inputs = tokens.astype(jnp.float32).reshape(N_DP, TOK_DEV, D)
    upstream = cotangent.astype(jnp.float32).reshape(N_DP, TOK_DEV, D)

    def one_pack(totals, pack_data):
        pack_rows, pack_grad, lengths = pack_data
        result, pullback = jax.vjp(lambda weights, values: layer(weights, values, lengths[0]), params, pack_rows)
        weight_grads, input_grad = pullback(pack_grad)
        totals = jax.tree.map(jnp.add, totals, weight_grads)
        return (totals, (result.astype(jnp.bfloat16), input_grad))
    empty_grads = jax.tree.map(jnp.zeros_like, params)
    totals, (outputs, input_grads) = lax.scan(one_pack, empty_grads, (inputs, upstream, seq_lengths))
    return (outputs.reshape(TOKENS, D), input_grads.reshape(TOKENS, D), totals[0], totals[1], totals[2], totals[3], totals[4], totals[5], totals[6], totals[7], totals[8], totals[9])
```

```python
import jax
import jax.numpy as jnp
from jax import lax
from jax.experimental import pallas as pl
from jax.experimental.pallas import tpu as pltpu
from jax.sharding import PartitionSpec as P

HD = 64
norm_eps = 1e-06
masked_score = -1000000000.0
bf16 = jnp.bfloat16
f32 = jnp.float32


def matmul(left, right):
    return jnp.dot(left, right, preferred_element_type=f32)


def contract_rows(left, right):
    return lax.dot_general(left, right, (((0,), (0,)), ((), ())), preferred_element_type=f32)


def contract_cols(left, right):
    return lax.dot_general(left, right, (((1,), (1,)), ((), ())), preferred_element_type=f32)


def normalize(values):
    factor = lax.rsqrt(jnp.mean(values * values, axis=-1, keepdims=True) + norm_eps)
    return (values * factor, factor)


def norm_backward(upstream, normed, factor, scaling):
    weighted = scaling * upstream
    inner = jnp.mean(weighted * normed, axis=-1, keepdims=True)
    return (factor * (weighted - normed * inner), jnp.sum(upstream * normed, axis=0))


def swap(block, axis, bit):
    count = lax.axis_size(axis)
    return lax.ppermute(block, axis, [(i, i ^ (1 << bit)) for i in range(count)])


def ring(block, step):
    count = lax.axis_size("tp")
    return lax.ppermute(block, "tp", [(i, (i + step) % count) for i in range(count)])


def pick(block, index, axis):
    return lax.dynamic_index_in_dim(block, index, axis, keepdims=False)


def rounded_sum(left, right):
    return (left.astype(f32) + right.astype(f32)).astype(bf16)


def gather_bits(block, bits, dp):
    for bit in bits:
        mine = (dp >> bit) & 1
        other = swap(block, "dp", bit)
        first = jnp.where(mine == 0, block, other)
        second = jnp.where(mine == 0, other, block)
        block = jnp.stack([first, second])
    return block


def halve(block, bit, axis, dp):
    mine = (dp >> bit) & 1
    keep = pick(block, mine, axis)
    send = pick(block, 1 - mine, axis)
    return rounded_sum(keep, swap(send, "dp", bit))


def forward_kernel(info, q_ref, k_ref, v_ref, o_ref, w_ref, bias_ref):
    rows, keys = bias_ref.shape

    @pl.when(pl.program_id(0) == 0)
    def _():
        row = lax.broadcasted_iota(jnp.int32, (rows, keys), 0) + info[0]
        col = lax.broadcasted_iota(jnp.int32, (rows, keys), 1)
        edge = info[1]
        same = (col >= edge).astype(jnp.int32) == (row >= edge).astype(jnp.int32)
        bias_ref[...] = jnp.where(same & (col <= row), 0.0, masked_score)

    outs = []
    for j in range(2):
        lanes = slice(j * HD, (j + 1) * HD)
        scores = contract_cols(q_ref[:, lanes], k_ref[:, lanes]) * (HD**-0.5) + bias_ref[...]
        top = jnp.max(scores, axis=-1, keepdims=True)
        shifted = jnp.exp(scores - top)
        total = jnp.sum(shifted, axis=-1, keepdims=True)
        weights = (shifted * (1.0 / total)).astype(bf16)
        w_ref[j] = weights
        outs.append(matmul(weights, v_ref[:, lanes]).astype(bf16))
    o_ref[...] = jnp.concatenate(outs, axis=1)


def backward_kernel(q_ref, k_ref, v_ref, g_ref, w_ref, dq_ref, dk_ref, dv_ref):
    dqs, dks, dvs = [], [], []
    for j in range(2):
        lanes = slice(j * HD, (j + 1) * HD)
        weights = w_ref[j]
        probs = weights.astype(f32)
        grad = g_ref[:, lanes]
        grad_weights = contract_cols(grad, v_ref[:, lanes])
        delta = jnp.sum(probs * grad_weights, axis=-1, keepdims=True)
        grad_scores = (probs * (grad_weights - delta)).astype(bf16)
        dqs.append((matmul(grad_scores, k_ref[:, lanes]) * (HD**-0.5)).astype(bf16))
        dks.append((contract_rows(grad_scores, q_ref[:, lanes]) * (HD**-0.5)).astype(bf16))
        dvs.append(contract_rows(weights, grad).astype(bf16))
    dq_ref[...] = jnp.concatenate(dqs, axis=1)
    dk_ref[...] = jnp.concatenate(dks, axis=1)
    dv_ref[...] = jnp.concatenate(dvs, axis=1)


def attend_forward(queries, keys, values, info):
    rows, width = queries.shape
    total = keys.shape[0]
    pairs = width // (2 * HD)
    small = pl.BlockSpec((rows, 2 * HD), lambda h, s: (0, h))
    large = pl.BlockSpec((total, 2 * HD), lambda h, s: (0, h))
    return pl.pallas_call(
        forward_kernel,
        grid_spec=pltpu.PrefetchScalarGridSpec(
            num_scalar_prefetch=1,
            grid=(pairs,),
            in_specs=[small, large, large],
            out_specs=[small, pl.BlockSpec((2, rows, total), lambda h, s: (h, 0, 0))],
            scratch_shapes=[pltpu.VMEM((rows, total), f32)],
        ),
        out_shape=[
            jax.ShapeDtypeStruct((rows, width), bf16),
            jax.ShapeDtypeStruct((2 * pairs, rows, total), bf16),
        ],
        name="attend_forward",
    )(info, queries, keys, values)


def attend_backward(queries, keys, values, grad, weights):
    rows, width = queries.shape
    total = keys.shape[0]
    pairs = width // (2 * HD)
    small = pl.BlockSpec((rows, 2 * HD), lambda h: (0, h))
    large = pl.BlockSpec((total, 2 * HD), lambda h: (0, h))
    return pl.pallas_call(
        backward_kernel,
        grid=(pairs,),
        in_specs=[small, large, large, small, pl.BlockSpec((2, rows, total), lambda h: (h, 0, 0))],
        out_specs=[small, large, large],
        out_shape=[
            jax.ShapeDtypeStruct((rows, width), bf16),
            jax.ShapeDtypeStruct((total, width), bf16),
            jax.ShapeDtypeStruct((total, width), bf16),
        ],
        name="attend_backward",
    )(queries, keys, values, grad, weights)


def local(
    tokens,
    cotangent,
    seq_lengths,
    attention_gain,
    query_weight,
    latent_down,
    key_up,
    value_up,
    out_weight,
    feedforward_gain,
    gate_weight,
    up_weight,
    down_weight,
):
    tp = lax.axis_index("tp")
    dp = lax.axis_index("dp")
    planes = lax.axis_size("tp")
    dp_count = lax.axis_size("dp")
    dp_bits = dp_count.bit_length() - 1
    core, xbit, ybit = (dp & 1, (dp >> 1) & 1, (dp >> 2) & 1)
    rows, model = tokens.shape
    lat_width, quarter = key_up.shape
    width = planes * quarter
    plane_of = [(tp + planes - k) % planes for k in range(planes)]
    boundary = seq_lengths[0, 0]

    def ring_gather(piece):
        got = [piece]
        for _ in range(planes - 1):
            got.append(ring(got[-1], 1))
        return got

    def in_order(pieces):
        block = jnp.zeros((planes,) + pieces[0].shape, pieces[0].dtype)
        for k in range(planes):
            block = lax.dynamic_update_index_in_dim(block, pieces[k], plane_of[k], 0)
        return block

    def ring_reduce(parts):
        total = parts[planes - 1]
        for k in range(planes - 2, -1, -1):
            total = ring(total.astype(bf16), -1).astype(f32) + parts[k].astype(f32)
        return total

    inputs = tokens.astype(f32)
    normed_one, factor_one = normalize(inputs)
    rows_one = (normed_one * attention_gain).astype(bf16)
    latent_own = matmul(rows_one, latent_down).astype(bf16)
    latents = in_order(ring_gather(latent_own)).reshape(planes * rows, 2 * lat_width)

    eighth = dp & 7
    q_rows, u_rows = model // 8, lat_width // 8
    q_piece = lax.dynamic_slice_in_dim(query_weight, eighth * q_rows, q_rows, 0)
    k_piece = lax.dynamic_slice_in_dim(key_up, eighth * u_rows, u_rows, 0)
    v_piece = lax.dynamic_slice_in_dim(value_up, eighth * u_rows, u_rows, 0)
    half_q = q_rows // 2
    packed = jnp.concatenate([q_piece[:half_q], k_piece, q_piece[half_q:], v_piece], axis=0)
    packed = in_order(ring_gather(packed))
    cut = half_q + u_rows
    side_a = gather_bits(packed[:, :cut], (1, 2, 0), dp)
    side_b = gather_bits(packed[:, cut:], (2, 1, 0), dp)
    side_a = side_a.transpose(1, 2, 0, 4, 3, 5)
    side_b = side_b.transpose(2, 1, 0, 4, 3, 5)
    query_full = jnp.concatenate([side_a[:, :, :, :half_q], side_b[:, :, :, :half_q]], axis=3)
    query_full = query_full.reshape(model, width)
    key_full = side_a[:, :, :, half_q:].reshape(lat_width, width)
    value_full = side_b[:, :, :, half_q:].reshape(lat_width, width)

    o_cols = model // 8
    o_piece = lax.dynamic_slice_in_dim(out_weight, eighth * o_cols, o_cols, 1)
    o_packed = in_order(ring_gather(o_piece))
    half_o = quarter // 2
    o_a = gather_bits(o_packed[:, :half_o], (1, 2, 0), dp).transpose(3, 4, 1, 2, 0, 5)
    o_b = gather_bits(o_packed[:, half_o:], (2, 1, 0), dp).transpose(3, 4, 2, 1, 0, 5)
    out_full = jnp.concatenate([o_a, o_b], axis=1).reshape(width, model)

    ff_quarter = gate_weight.shape[1]
    ff_half = ff_quarter // 2
    ff_pad = -(-ff_half // 128) * 128

    def core_half(block):
        chosen = jnp.where(core == 0, block[:, :ff_half], block[:, ff_half:])
        return jnp.pad(chosen, ((0, 0), (0, ff_pad - ff_half)))

    down_half = lax.dynamic_slice_in_dim(down_weight, core * ff_half, ff_half, 0)
    down_turned = jnp.pad(down_half.T, ((0, 0), (0, ff_pad - ff_half)))
    ff_own = jnp.concatenate([core_half(gate_weight), core_half(up_weight), down_turned], axis=1)
    spot = (dp >> 1) & 3
    turned_spot = xbit * 2 + ybit
    ff_rows = model // 8
    ff_a = lax.dynamic_slice_in_dim(ff_own, spot * ff_rows, ff_rows, 0)
    ff_b = lax.dynamic_slice_in_dim(ff_own, model // 2 + turned_spot * ff_rows, ff_rows, 0)
    ff_pieces = ring_gather(jnp.concatenate([ff_a, ff_b], axis=0))
    ff_weights = [ff_own]
    for k in range(1, planes):
        top = gather_bits(ff_pieces[k][:ff_rows], (1, 2), dp).reshape(model // 2, 3 * ff_pad)
        bottom = gather_bits(ff_pieces[k][ff_rows:], (2, 1), dp).reshape(model // 2, 3 * ff_pad)
        ff_weights.append(jnp.concatenate([top, bottom], axis=0))

    queries = matmul(rows_one, query_full).astype(bf16)
    group = width // 2
    keys = jnp.concatenate(
        [
            matmul(latents[:, g * lat_width : (g + 1) * lat_width], key_full[:, g * group : (g + 1) * group]).astype(bf16)
            for g in range(2)
        ],
        axis=1,
    )
    values = jnp.concatenate(
        [
            matmul(latents[:, g * lat_width : (g + 1) * lat_width], value_full[:, g * group : (g + 1) * group]).astype(bf16)
            for g in range(2)
        ],
        axis=1,
    )
    info = jnp.stack([tp.astype(jnp.int32) * rows, boundary])
    attended, weights = attend_forward(queries, keys, values, info)
    mixed = inputs + matmul(attended, out_full)
    normed_two, factor_two = normalize(mixed)
    rows_two = (normed_two * feedforward_gain).astype(bf16)

    both_two = jnp.concatenate([rows_two, swap(rows_two, "dp", 0)], axis=0)
    both_up = jnp.concatenate([cotangent, swap(cotangent, "dp", 0)], axis=0)
    out_sum = 0.0
    grad_sum = 0.0
    ff_grads = []
    for k in range(planes):
        packed_w = ff_weights[k]
        gate_up = packed_w[:, : 2 * ff_pad]
        down_t = packed_w[:, 2 * ff_pad :]
        hidden = matmul(both_two, gate_up)
        gate, up = hidden[:, :ff_pad], hidden[:, ff_pad:]
        sigmoid = jax.nn.sigmoid(gate)
        silu = gate * sigmoid
        act = (silu * up).astype(bf16)
        grad_act = matmul(both_up, down_t)
        grad_gate = (grad_act * up * sigmoid * (1.0 + gate * (1.0 - sigmoid))).astype(bf16)
        grad_up = (grad_act * silu).astype(bf16)
        grad_hidden = jnp.concatenate([grad_gate, grad_up], axis=1)
        out_sum = out_sum + contract_cols(act, down_t)
        grad_sum = grad_sum + contract_cols(grad_hidden, gate_up)
        ff_grads.append(
            jnp.concatenate(
                [contract_rows(both_two, grad_hidden).astype(bf16), contract_rows(both_up, act).astype(bf16)],
                axis=1,
            )
        )
    output = (
        mixed + out_sum[:rows] + swap(out_sum[rows:].astype(bf16), "dp", 0).astype(f32)
    ).astype(bf16)
    grad_two = grad_sum[:rows] + swap(grad_sum[rows:].astype(bf16), "dp", 0).astype(f32)
    back_two, gain_two = norm_backward(grad_two, normed_two, factor_two, feedforward_gain)
    grad_mixed = cotangent.astype(f32) + back_two

    high = dp_count // 8

    def high_bits(block):
        for bit in range(dp_bits - 1, 2, -1):
            block = block.reshape((2, -1) + block.shape[1:])
            block = halve(block, bit, 0, dp)
        return block.reshape(block.shape[1:])

    def sum_ff(block):
        part = model // dp_count
        block = high_bits(block.reshape(high, 2, 2, 2, part, 3 * ff_pad))
        side_a = halve(halve(block[:, :, 0], 1, 1, dp), 2, 0, dp)
        side_b = halve(halve(block[:, :, 1], 2, 0, dp), 1, 0, dp)
        return jnp.stack([side_a, side_b])

    ff_total = ring_reduce([sum_ff(block) for block in ff_grads])
    ff_mine = pick(ff_total, core, 0)
    ff_other = swap(pick(ff_total, 1 - core, 0), "dp", 0)
    ff_first = jnp.where(core == 0, ff_mine, ff_other)
    ff_second = jnp.where(core == 0, ff_other, ff_mine)

    def joined(index):
        lanes = slice(index * ff_pad, index * ff_pad + ff_half)
        return jnp.concatenate([ff_first[:, lanes], ff_second[:, lanes]], axis=1)

    gate_grad, up_grad, down_grad = joined(0), joined(1), joined(2).T

    def sum_attention(blocks):
        lanes = blocks[0].shape[-1]
        part = blocks[0].shape[1]
        block = jnp.stack(blocks, axis=1)
        block = high_bits(block.reshape(high, 2, 2, 2, planes, part, lanes))
        block = halve(block, 0, 2, dp)
        cut = lanes // 2
        side_a = halve(halve(block[..., :cut], 1, 1, dp), 2, 0, dp)
        side_b = halve(halve(block[..., cut:], 2, 0, dp), 1, 0, dp)
        both = jnp.concatenate([side_a, side_b], axis=-1)
        return ring_reduce([both[k] for k in range(planes)])

    def columns_of(block, k, size):
        return lax.dynamic_slice_in_dim(block, plane_of[k] * size, size, 1)

    part = model // dp_count
    mixed_rows = grad_mixed.astype(bf16)
    out_grad = sum_attention(
        [
            contract_rows(mixed_rows, columns_of(attended, k, quarter)).astype(bf16).reshape(dp_count, part, quarter)
            for k in range(planes)
        ]
    ).T

    grad_attended = contract_cols(mixed_rows, out_full).astype(bf16)
    grad_queries, grad_keys, grad_values = attend_backward(queries, keys, values, grad_attended, weights)
    latent_part = jnp.concatenate(
        [
            contract_cols(grad_keys[:, g * group : (g + 1) * group], key_full[:, g * group : (g + 1) * group])
            + contract_cols(grad_values[:, g * group : (g + 1) * group], value_full[:, g * group : (g + 1) * group])
            for g in range(2)
        ],
        axis=1,
    ).astype(bf16)
    grad_latent = ring_reduce(
        [lax.dynamic_slice_in_dim(latent_part, plane_of[k] * rows, rows, 0) for k in range(planes)]
    ).astype(bf16)

    up_part = lat_width // dp_count
    lane = 2 * quarter * up_part // part

    def late_block(k):
        of_query = contract_rows(rows_one, columns_of(grad_queries, k, quarter)).astype(bf16)
        lat_k = lax.dynamic_slice_in_dim(latents, (plane_of[k] * 2 // planes) * lat_width, lat_width, 1)
        both = jnp.concatenate([columns_of(grad_keys, k, quarter), columns_of(grad_values, k, quarter)], axis=1)
        of_up = contract_rows(lat_k, both).astype(bf16).reshape(dp_count, up_part, 2 * quarter)
        of_up = jnp.concatenate([of_up[:, :, i : i + lane] for i in range(0, 2 * quarter, lane)], axis=1)
        return jnp.concatenate([of_query.reshape(dp_count, part, quarter), of_up], axis=2)

    late = sum_attention([late_block(k) for k in range(planes)])
    query_grad = late[:, :quarter]
    up_both = late[:, quarter:].reshape(-1, up_part, lane)
    up_both = jnp.concatenate([up_both[i] for i in range(up_both.shape[0])], axis=1)
    key_grad, value_grad = up_both[:, :quarter], up_both[:, quarter:]

    lat_cols = 2 * lat_width // planes
    latent_grad = sum_attention(
        [
            contract_rows(rows_one, columns_of(grad_latent, k, lat_cols)).astype(bf16).reshape(dp_count, part, lat_cols)
            for k in range(planes)
        ]
    )
    grad_one = contract_cols(grad_queries, query_full) + contract_cols(grad_latent, latent_down)
    back_one, gain_one = norm_backward(grad_one, normed_one, factor_one, attention_gain)
    tokens_grad = grad_mixed + back_one

    gains = jnp.stack([gain_one, gain_two]).reshape(2, dp_count, part)
    for bit in range(dp_bits - 1, -1, -1):
        gains = gains.reshape(2, 2, gains.shape[1] // 2, part)
        mine = (dp >> bit) & 1
        gains = pick(gains, mine, 1) + swap(pick(gains, 1 - mine, 1), "dp", bit)
    gains = gains.reshape(2, part)
    for bit in range(planes.bit_length() - 1):
        gains = gains + swap(gains, "tp", bit)
    return (
        output,
        tokens_grad,
        gains[0],
        query_grad,
        latent_grad,
        key_grad,
        value_grad,
        out_grad,
        gains[1],
        gate_grad,
        up_grad,
        down_grad,
    )


def solution(mesh):
    return jax.shard_map(
        local,
        mesh=mesh,
        in_specs=(
            P(("dp", "tp"), None),
            P(("dp", "tp"), None),
            P("dp", None),
            P(),
            P(None, "tp"),
            P(),
            P(None, "tp"),
            P(None, "tp"),
            P("tp", None),
            P(),
            P(None, "tp"),
            P(None, "tp"),
            P("tp", None),
        ),
        out_specs=(
            P(("dp", "tp"), None),
            P(("dp", "tp"), None),
            P("dp"),
            P("dp", "tp"),
            P("dp", "tp"),
            P("dp", "tp"),
            P("dp", "tp"),
            P("tp", "dp"),
            P("dp"),
            P("dp", "tp"),
            P("dp", "tp"),
            P("tp", "dp"),
        ),
        check_vma=False,
    )
```

```python
import jax
import jax.numpy as jnp
from jax import lax
from jax.experimental import pallas as pl
from jax.experimental.pallas import tpu as pltpu
from jax.sharding import PartitionSpec as P

HD = 64
norm_eps = 1e-06
masked_score = -1000000000.0
bf16 = jnp.bfloat16
f32 = jnp.float32


def matmul(left, right):
    return jnp.dot(left, right, preferred_element_type=f32)


def contract_rows(left, right):
    return lax.dot_general(left, right, (((0,), (0,)), ((), ())), preferred_element_type=f32)


def contract_cols(left, right):
    return lax.dot_general(left, right, (((1,), (1,)), ((), ())), preferred_element_type=f32)


def normalize(values):
    factor = lax.rsqrt(jnp.mean(values * values, axis=-1, keepdims=True) + norm_eps)
    return (values * factor, factor)


def norm_backward(upstream, normed, factor, scaling):
    weighted = scaling * upstream
    inner = jnp.mean(weighted * normed, axis=-1, keepdims=True)
    return (factor * (weighted - normed * inner), jnp.sum(upstream * normed, axis=0))


def swap(block, axis, bit):
    count = lax.axis_size(axis)
    return lax.ppermute(block, axis, [(i, i ^ (1 << bit)) for i in range(count)])


def ring(block, step):
    count = lax.axis_size("tp")
    return lax.ppermute(block, "tp", [(i, (i + step) % count) for i in range(count)])


def pick(block, index, axis):
    return lax.dynamic_index_in_dim(block, index, axis, keepdims=False)


def rounded_sum(left, right):
    return (left.astype(f32) + right.astype(f32)).astype(bf16)


def gather_bits(block, bits, dp):
    for bit in bits:
        mine = (dp >> bit) & 1
        other = swap(block, "dp", bit)
        first = jnp.where(mine == 0, block, other)
        second = jnp.where(mine == 0, other, block)
        block = jnp.stack([first, second])
    return block


def halve(block, bit, axis, dp):
    mine = (dp >> bit) & 1
    keep = pick(block, mine, axis)
    send = pick(block, 1 - mine, axis)
    return rounded_sum(keep, swap(send, "dp", bit))


def forward_kernel(info, q_ref, k_ref, v_ref, o_ref, w_ref, bias_ref):
    rows, keys = bias_ref.shape

    @pl.when(pl.program_id(0) == 0)
    def _():
        edge = info[0]
        for k in range(keys // rows):
            row = lax.broadcasted_iota(jnp.int32, (rows, rows), 0) + info[1]
            col = lax.broadcasted_iota(jnp.int32, (rows, rows), 1) + info[1 + k]
            same = (col >= edge).astype(jnp.int32) == (row >= edge).astype(jnp.int32)
            bias_ref[:, k * rows : (k + 1) * rows] = jnp.where(same & (col <= row), 0.0, masked_score)

    outs = []
    for j in range(2):
        lanes = slice(j * HD, (j + 1) * HD)
        scores = contract_cols(q_ref[:, lanes], k_ref[:, lanes]) * (HD**-0.5) + bias_ref[...]
        top = jnp.max(scores, axis=-1, keepdims=True)
        shifted = jnp.exp(scores - top)
        total = jnp.sum(shifted, axis=-1, keepdims=True)
        weights = (shifted * (1.0 / total)).astype(bf16)
        w_ref[j] = weights
        outs.append(matmul(weights, v_ref[:, lanes]).astype(bf16))
    o_ref[...] = jnp.concatenate(outs, axis=1)


def backward_kernel(q_ref, k_ref, v_ref, g_ref, w_ref, dq_ref, dk_ref, dv_ref):
    dqs, dks, dvs = [], [], []
    for j in range(2):
        lanes = slice(j * HD, (j + 1) * HD)
        weights = w_ref[j]
        probs = weights.astype(f32)
        grad = g_ref[:, lanes]
        grad_weights = contract_cols(grad, v_ref[:, lanes])
        delta = jnp.sum(probs * grad_weights, axis=-1, keepdims=True)
        grad_scores = (probs * (grad_weights - delta)).astype(bf16)
        dqs.append((matmul(grad_scores, k_ref[:, lanes]) * (HD**-0.5)).astype(bf16))
        dks.append((contract_rows(grad_scores, q_ref[:, lanes]) * (HD**-0.5)).astype(bf16))
        dvs.append(contract_rows(weights, grad).astype(bf16))
    dq_ref[...] = jnp.concatenate(dqs, axis=1)
    dk_ref[...] = jnp.concatenate(dks, axis=1)
    dv_ref[...] = jnp.concatenate(dvs, axis=1)


def attend_forward(queries, keys, values, info):
    rows, width = queries.shape
    total = keys.shape[0]
    pairs = width // (2 * HD)
    small = pl.BlockSpec((rows, 2 * HD), lambda h, s: (0, h))
    large = pl.BlockSpec((total, 2 * HD), lambda h, s: (0, h))
    return pl.pallas_call(
        forward_kernel,
        grid_spec=pltpu.PrefetchScalarGridSpec(
            num_scalar_prefetch=1,
            grid=(pairs,),
            in_specs=[small, large, large],
            out_specs=[small, pl.BlockSpec((2, rows, total), lambda h, s: (h, 0, 0))],
            scratch_shapes=[pltpu.VMEM((rows, total), f32)],
        ),
        out_shape=[
            jax.ShapeDtypeStruct((rows, width), bf16),
            jax.ShapeDtypeStruct((2 * pairs, rows, total), bf16),
        ],
        name="attend_forward",
    )(info, queries, keys, values)


def attend_backward(queries, keys, values, grad, weights):
    rows, width = queries.shape
    total = keys.shape[0]
    pairs = width // (2 * HD)
    small = pl.BlockSpec((rows, 2 * HD), lambda h: (0, h))
    large = pl.BlockSpec((total, 2 * HD), lambda h: (0, h))
    return pl.pallas_call(
        backward_kernel,
        grid=(pairs,),
        in_specs=[small, large, large, small, pl.BlockSpec((2, rows, total), lambda h: (h, 0, 0))],
        out_specs=[small, large, large],
        out_shape=[
            jax.ShapeDtypeStruct((rows, width), bf16),
            jax.ShapeDtypeStruct((total, width), bf16),
            jax.ShapeDtypeStruct((total, width), bf16),
        ],
        name="attend_backward",
    )(queries, keys, values, grad, weights)


def feed_kernel(x_ref, g_ref, w_ref, dh_ref, act_ref, out_ref, dx_ref):
    pad = act_ref.shape[2]
    weights = w_ref[0]
    gate_up = weights[:, : 2 * pad]
    down_t = weights[:, 2 * pad :]
    hidden = matmul(x_ref[...], gate_up)
    gate, up = hidden[:, :pad], hidden[:, pad:]
    sigmoid = jax.nn.sigmoid(gate)
    silu = gate * sigmoid
    act = (silu * up).astype(bf16)
    act_ref[0] = act
    grad_act = matmul(g_ref[...], down_t)
    grad_gate = (grad_act * up * sigmoid * (1.0 + gate * (1.0 - sigmoid))).astype(bf16)
    grad_up = (grad_act * silu).astype(bf16)
    grad_hidden = jnp.concatenate([grad_gate, grad_up], axis=1)
    dh_ref[0] = grad_hidden

    @pl.when(pl.program_id(0) == 0)
    def _():
        out_ref[...] = jnp.zeros_like(out_ref)
        dx_ref[...] = jnp.zeros_like(dx_ref)

    out_ref[...] += contract_cols(act, down_t)
    dx_ref[...] += contract_cols(grad_hidden, gate_up)


def feed_forward(both_two, both_up, weights):
    count, model, lanes = weights.shape
    rows = both_two.shape[0]
    pad = lanes // 3
    whole = pl.BlockSpec((rows, model), lambda k: (0, 0))
    return pl.pallas_call(
        feed_kernel,
        grid=(count,),
        in_specs=[whole, whole, pl.BlockSpec((1, model, lanes), lambda k: (k, 0, 0))],
        out_specs=[
            pl.BlockSpec((1, rows, 2 * pad), lambda k: (k, 0, 0)),
            pl.BlockSpec((1, rows, pad), lambda k: (k, 0, 0)),
            whole,
            whole,
        ],
        out_shape=[
            jax.ShapeDtypeStruct((count, rows, 2 * pad), bf16),
            jax.ShapeDtypeStruct((count, rows, pad), bf16),
            jax.ShapeDtypeStruct((rows, model), f32),
            jax.ShapeDtypeStruct((rows, model), f32),
        ],
        name="feed_forward",
    )(both_two, both_up, weights)


def feed_grad_kernel(spots, xa_ref, xb_ref, ga_ref, gb_ref, dh_ref, act_ref, out_ref):
    pad = act_ref.shape[2]
    left = jnp.concatenate([xa_ref[...], xb_ref[...]], axis=1)
    out_ref[0, :, : 2 * pad] = contract_rows(left, dh_ref[0]).astype(bf16)
    left = jnp.concatenate([ga_ref[...], gb_ref[...]], axis=1)
    out_ref[0, :, 2 * pad :] = contract_rows(left, act_ref[0]).astype(bf16)


def feed_grads(spots, both_two, both_up, grad_hidden, act):
    rows, model = both_two.shape
    count, _, pad = act.shape
    block = model // 8
    first = pl.BlockSpec((rows, block), lambda k, s: (0, s[0]))
    second = pl.BlockSpec((rows, block), lambda k, s: (0, s[1]))
    return pl.pallas_call(
        feed_grad_kernel,
        grid_spec=pltpu.PrefetchScalarGridSpec(
            num_scalar_prefetch=1,
            grid=(count,),
            in_specs=[
                first,
                second,
                first,
                second,
                pl.BlockSpec((1, rows, 2 * pad), lambda k, s: (k, 0, 0)),
                pl.BlockSpec((1, rows, pad), lambda k, s: (k, 0, 0)),
            ],
            out_specs=pl.BlockSpec((1, 2 * block, 3 * pad), lambda k, s: (k, 0, 0)),
        ),
        out_shape=jax.ShapeDtypeStruct((count, 2 * block, 3 * pad), bf16),
        name="feed_grads",
    )(spots, both_two, both_two, both_up, both_up, grad_hidden, act)


def local(
    tokens,
    cotangent,
    seq_lengths,
    attention_gain,
    query_weight,
    latent_down,
    key_up,
    value_up,
    out_weight,
    feedforward_gain,
    gate_weight,
    up_weight,
    down_weight,
):
    tp = lax.axis_index("tp")
    dp = lax.axis_index("dp")
    planes = lax.axis_size("tp")
    dp_count = lax.axis_size("dp")
    dp_bits = dp_count.bit_length() - 1
    core, xbit, ybit = (dp & 1, (dp >> 1) & 1, (dp >> 2) & 1)
    eighth = dp & 7
    rows, model = tokens.shape
    lat_width, quarter = key_up.shape
    width = planes * quarter
    high = dp_count // 8
    part = model // dp_count
    block = model // 8
    up_part = lat_width // dp_count
    plane_of = [(tp + planes - k) % planes for k in range(planes)]
    boundary = seq_lengths[0, 0]

    def ring_gather(piece):
        got = [piece]
        for _ in range(planes - 1):
            got.append(ring(got[-1], 1))
        return got

    def ring_reduce(parts):
        total = parts[planes - 1]
        for k in range(planes - 2, -1, -1):
            total = ring(total.astype(bf16), -1).astype(f32) + parts[k].astype(f32)
        return total

    def blocks_first(array):
        if high == 1:
            return array
        shaped = array.reshape(array.shape[0], high, 8, part)
        return shaped.transpose(0, 2, 1, 3).reshape(array.shape)

    q_piece = lax.dynamic_slice_in_dim(query_weight, eighth * block, block, 0)
    q_got = jnp.stack(ring_gather(q_piece))

    inputs = tokens.astype(f32)
    normed_one, factor_one = normalize(inputs)
    rows_one = (normed_one * attention_gain).astype(bf16)
    latent_own = matmul(rows_one, latent_down).astype(bf16)
    up_piece = jnp.where(core == 0, key_up, value_up)
    lat_up = jnp.concatenate([latent_own, up_piece], axis=1)
    lat_got = ring_gather(lat_up)
    latents = jnp.concatenate([got[:, : 2 * lat_width] for got in lat_got], axis=0)
    up_mine = jnp.concatenate([got[:, 2 * lat_width :] for got in lat_got], axis=1)
    up_other = swap(up_mine, "dp", 0)
    keys_up = jnp.where(core == 0, up_mine, up_other)
    values_up = jnp.where(core == 0, up_other, up_mine)
    groups = [plane_of[k] * 2 // planes for k in range(planes)]
    group_row = jnp.concatenate(
        [jnp.full((1, quarter), 1, jnp.int32) * groups[k].astype(jnp.int32) for k in range(planes)], axis=1
    )

    def both_groups(array):
        zero = jnp.zeros_like(array)
        return jnp.concatenate([jnp.where(group_row == g, array, zero) for g in range(2)], axis=0)

    keys_wide, values_wide = both_groups(keys_up), both_groups(values_up)

    q_all = gather_bits(q_got, (1, 2, 0), dp)
    query_full = q_all.transpose(1, 2, 0, 4, 3, 5).reshape(model, width)

    gate_weight, up_weight, down_weight, out_weight, _ = lax.optimization_barrier(
        (gate_weight, up_weight, down_weight, out_weight, lat_got[1])
    )
    ff_half = gate_weight.shape[1] // 2
    ff_pad = -(-ff_half // 128) * 128

    def core_half(array):
        chosen = jnp.where(core == 0, array[:, :ff_half], array[:, ff_half:])
        return jnp.pad(chosen, ((0, 0), (0, ff_pad - ff_half)))

    down_half = lax.dynamic_slice_in_dim(down_weight, core * ff_half, ff_half, 0)
    down_turned = jnp.pad(down_half.T, ((0, 0), (0, ff_pad - ff_half)))
    ff_own = jnp.concatenate([core_half(gate_weight), core_half(up_weight), down_turned], axis=1)
    spot = (dp >> 1) & 3
    turned_spot = xbit * 2 + ybit
    ff_a = lax.dynamic_slice_in_dim(ff_own, spot * block, block, 0)
    ff_b = lax.dynamic_slice_in_dim(ff_own, model // 2 + turned_spot * block, block, 0)
    ff_pieces = ring_gather(jnp.concatenate([ff_a, ff_b], axis=0))
    ff_weights = [ff_own]
    for k in range(1, planes):
        top = gather_bits(ff_pieces[k][:block], (1, 2), dp).reshape(model // 2, 3 * ff_pad)
        bottom = gather_bits(ff_pieces[k][block:], (2, 1), dp).reshape(model // 2, 3 * ff_pad)
        ff_weights.append(jnp.concatenate([top, bottom], axis=0))
    ff_weights = jnp.stack(ff_weights)

    o_piece = lax.dynamic_slice_in_dim(out_weight, eighth * block, block, 1)
    o_got = gather_bits(jnp.concatenate(ring_gather(o_piece), axis=0), (1, 2, 0), dp)
    out_full = o_got.transpose(3, 1, 2, 0, 4).reshape(width, model)

    queries = matmul(rows_one, query_full).astype(bf16)
    keys = matmul(latents, keys_wide).astype(bf16)
    values = matmul(latents, values_wide).astype(bf16)
    info = jnp.stack([boundary] + [plane_of[k].astype(jnp.int32) * rows for k in range(planes)])
    attended, weights = attend_forward(queries, keys, values, info)
    mixed = inputs + matmul(attended, out_full)
    normed_two, factor_two = normalize(mixed)
    rows_two = (normed_two * feedforward_gain).astype(bf16)

    both_two = jnp.concatenate([rows_two, swap(rows_two, "dp", 0)], axis=0)
    both_up = jnp.concatenate([cotangent, swap(cotangent, "dp", 0)], axis=0)
    grad_hidden, act, out_sum, grad_sum = feed_forward(both_two, both_up, ff_weights)
    grad_two = grad_sum[:rows] + swap(grad_sum[rows:].astype(bf16), "dp", 0).astype(f32)
    back_two, gain_two = norm_backward(grad_two, normed_two, factor_two, feedforward_gain)
    grad_mixed = cotangent.astype(f32) + back_two
    output = (
        mixed + out_sum[:rows] + swap(out_sum[rows:].astype(bf16), "dp", 0).astype(f32)
    ).astype(bf16)

    lefts = (blocks_first(both_two), blocks_first(both_up))

    def ff_blocks(first, second):
        spots = jnp.stack([eighth ^ first, eighth ^ second]).astype(jnp.int32)
        return feed_grads(spots, *lefts, grad_hidden, act)

    def high_bits(array):
        for bit in range(dp_bits - 1, 2, -1):
            array = array.reshape((2, -1) + array.shape[1:])
            array = halve(array, bit, 0, dp)
        return array.reshape(array.shape[1:])

    def ff_step(keep, got, bit):
        rest = swap(rounded_sum(keep[:, block:], got[:, block:]), "dp", bit)
        return rounded_sum(rounded_sum(keep[:, :block], got[:, :block]), rest)

    got_a = swap(ff_blocks(2, 6), "dp", 1)
    got_b = swap(ff_blocks(5, 7), "dp", 2)
    side_a = ff_step(ff_blocks(0, 4), got_a, 2)
    side_b = ff_step(ff_blocks(1, 3), got_b, 1)
    if high > 1:
        both = jnp.stack([side_a, side_b], axis=2).reshape(planes, high, part, 2, 3 * ff_pad)
        both = high_bits(both.transpose(1, 2, 0, 3, 4))
        side_a, side_b = both[:, :, 0].transpose(1, 0, 2), both[:, :, 1].transpose(1, 0, 2)
    ff_total = ring_reduce([jnp.stack([side_a[k], side_b[k]]) for k in range(planes)])
    ff_mine = ff_total[0]
    ff_other = swap(ff_total[1], "dp", 0)
    ff_first = jnp.where(core == 0, ff_mine, ff_other)
    ff_second = jnp.where(core == 0, ff_other, ff_mine)

    def joined(index):
        lanes = slice(index * ff_pad, index * ff_pad + ff_half)
        return jnp.concatenate([ff_first[:, lanes], ff_second[:, lanes]], axis=1)

    gate_grad, up_grad, down_grad = joined(0), joined(1), joined(2).T

    near = (0, 4, 2, 6)
    far = (1, 5, 3, 7)

    def columns(array, blocks):
        array = blocks_first(array)
        return jnp.concatenate(
            [lax.dynamic_slice_in_dim(array, (eighth ^ b) * block, block, 1) for b in blocks], axis=1
        )

    def block_rows(array, blocks):
        shaped = array.reshape(high, 8, up_part, array.shape[1])
        return jnp.stack(
            [pick(shaped, eighth ^ b, 1).reshape(high * up_part, array.shape[1]) for b in blocks]
        )

    def halvings(keep, send):
        total = rounded_sum(keep, swap(send, "dp", 0))
        total = rounded_sum(total[:2], swap(total[2:], "dp", 1))
        return rounded_sum(total[0], swap(total[1], "dp", 2))

    mixed_rows = grad_mixed.astype(bf16)
    out_part = contract_rows(mixed_rows, attended).astype(bf16)
    out_part = lax.psum_scatter(out_part, "dp", scatter_dimension=0, tiled=True)
    out_grad = ring_reduce([out_part[:, k * quarter : (k + 1) * quarter] for k in range(planes)]).T

    grad_attended = contract_cols(mixed_rows, out_full).astype(bf16)
    grad_queries, grad_keys, grad_values = attend_backward(queries, keys, values, grad_attended, weights)
    latent_part = (contract_cols(grad_keys, keys_wide) + contract_cols(grad_values, values_wide)).astype(bf16)
    grad_latent = ring_reduce([latent_part[k * rows : (k + 1) * rows] for k in range(planes)]).astype(bf16)

    def one_group(array):
        return jnp.where(group_row == 0, array[:lat_width], array[lat_width:])

    key_part = one_group(contract_rows(latents, grad_keys)).astype(bf16)
    value_part = one_group(contract_rows(latents, grad_values)).astype(bf16)
    one_near, one_far = columns(rows_one, near), columns(rows_one, far)

    def late(left, blocks):
        of_query = contract_rows(left, grad_queries).astype(bf16).reshape(4, block, width)
        return jnp.concatenate([of_query, block_rows(key_part, blocks), block_rows(value_part, blocks)], axis=1)

    late_sum = halvings(late(one_near, near), late(one_far, far))
    if high > 1:
        cuts = [late_sum[:block], late_sum[block : block + lat_width // 8], late_sum[block + lat_width // 8 :]]
        late_sum = high_bits(jnp.concatenate([cut.reshape(high, -1, width) for cut in cuts], axis=1))
    late_sum = ring_reduce([late_sum[:, k * quarter : (k + 1) * quarter] for k in range(planes)])
    query_grad = late_sum[:part]
    key_grad = late_sum[part : part + up_part]
    value_grad = late_sum[part + up_part :]

    grad_one = contract_cols(grad_queries, query_full) + contract_cols(grad_latent, latent_down)
    back_one, gain_one = norm_backward(grad_one, normed_one, factor_one, attention_gain)
    tokens_grad = grad_mixed + back_one

    gains = jnp.stack([gain_one, gain_two])

    def last(left, blocks):
        extra = jnp.pad(columns(gains, blocks).T.astype(bf16), ((0, 0), (0, 126)))
        both = jnp.concatenate([contract_rows(left, grad_latent).astype(bf16), extra], axis=1)
        return both.reshape(4, block, both.shape[1])

    last_sum = halvings(last(one_near, near), last(one_far, far))
    if high > 1:
        last_sum = high_bits(last_sum.reshape(high, part, last_sum.shape[1]))
    lat_cols = 2 * lat_width // planes
    last_sum = ring_reduce(
        [
            jnp.concatenate(
                [
                    lax.dynamic_slice_in_dim(last_sum, plane_of[k] * lat_cols, lat_cols, 1),
                    last_sum[:, 2 * lat_width :],
                ],
                axis=1,
            )
            for k in range(planes)
        ]
    )
    latent_grad = last_sum[:, :lat_cols]
    return (
        output,
        tokens_grad,
        last_sum[:, lat_cols],
        query_grad,
        latent_grad,
        key_grad,
        value_grad,
        out_grad,
        last_sum[:, lat_cols + 1],
        gate_grad,
        up_grad,
        down_grad,
    )


def solution(mesh):
    return jax.shard_map(
        local,
        mesh=mesh,
        in_specs=(
            P(("dp", "tp"), None),
            P(("dp", "tp"), None),
            P("dp", None),
            P(),
            P(None, "tp"),
            P(),
            P(None, "tp"),
            P(None, "tp"),
            P("tp", None),
            P(),
            P(None, "tp"),
            P(None, "tp"),
            P("tp", None),
        ),
        out_specs=(
            P(("dp", "tp"), None),
            P(("dp", "tp"), None),
            P("dp"),
            P("dp", "tp"),
            P("dp", "tp"),
            P("dp", "tp"),
            P("dp", "tp"),
            P("tp", "dp"),
            P("dp"),
            P("dp", "tp"),
            P("dp", "tp"),
            P("tp", "dp"),
        ),
        check_vma=False,
    )
```

```python
import functools

import jax
import jax.numpy as jnp
from jax import lax
from jax.experimental import pallas as pl
from jax.experimental.pallas import tpu as pltpu
from jax.sharding import PartitionSpec as P


HD = 64
norm_eps = 1e-06
masked_score = -1000000000.0
bf16 = jnp.bfloat16
f32 = jnp.float32


def matmul(left, right):
    return jnp.dot(left, right, preferred_element_type=f32)


def contract_rows(left, right):
    return lax.dot_general(left, right, (((0,), (0,)), ((), ())), preferred_element_type=f32)


def contract_cols(left, right):
    return lax.dot_general(left, right, (((1,), (1,)), ((), ())), preferred_element_type=f32)


def normalize(values):
    factor = lax.rsqrt(jnp.mean(values * values, axis=-1, keepdims=True) + norm_eps)
    return (values * factor, factor)


def norm_backward(upstream, normed, factor, scaling):
    weighted = scaling * upstream
    inner = jnp.mean(weighted * normed, axis=-1, keepdims=True)
    return (factor * (weighted - normed * inner), jnp.sum(upstream * normed, axis=0))


def swap(block, axis, bit):
    count = lax.axis_size(axis)
    return lax.ppermute(block, axis, [(i, i ^ (1 << bit)) for i in range(count)])


def ring(block, step):
    count = lax.axis_size("tp")
    return lax.ppermute(block, "tp", [(i, (i + step) % count) for i in range(count)])


def pick(block, index, axis):
    return lax.dynamic_index_in_dim(block, index, axis, keepdims=False)


def rounded_sum(left, right):
    return (left.astype(f32) + right.astype(f32)).astype(bf16)


def gather_bits(block, bits, dp):
    for bit in bits:
        mine = (dp >> bit) & 1
        other = swap(block, "dp", bit)
        first = jnp.where(mine == 0, block, other)
        second = jnp.where(mine == 0, other, block)
        block = jnp.stack([first, second])
    return block


def halve(block, bit, axis, dp):
    mine = (dp >> bit) & 1
    keep = pick(block, mine, axis)
    send = pick(block, 1 - mine, axis)
    return rounded_sum(keep, swap(send, "dp", bit))


def forward_kernel(info, q_ref, k_ref, v_ref, o_ref, w_ref, bias_ref):
    rows, keys = bias_ref.shape

    @pl.when(pl.program_id(0) == 0)
    def _():
        edge = info[0]
        for k in range(keys // rows):
            row = lax.broadcasted_iota(jnp.int32, (rows, rows), 0) + info[1]
            col = lax.broadcasted_iota(jnp.int32, (rows, rows), 1) + info[1 + k]
            same = (col >= edge).astype(jnp.int32) == (row >= edge).astype(jnp.int32)
            bias_ref[:, k * rows : (k + 1) * rows] = jnp.where(same & (col <= row), 0.0, masked_score)

    outs = []
    for j in range(2):
        lanes = slice(j * HD, (j + 1) * HD)
        scores = contract_cols(q_ref[:, lanes], k_ref[:, lanes]) * (HD**-0.5) + bias_ref[...]
        top = jnp.max(scores, axis=-1, keepdims=True)
        shifted = jnp.exp(scores - top)
        total = jnp.sum(shifted, axis=-1, keepdims=True)
        weights = (shifted * (1.0 / total)).astype(bf16)
        w_ref[j] = weights
        outs.append(matmul(weights, v_ref[:, lanes]).astype(bf16))
    o_ref[...] = jnp.concatenate(outs, axis=1)


def backward_kernel(q_ref, k_ref, v_ref, g_ref, w_ref, dq_ref, dk_ref, dv_ref):
    dqs, dks, dvs = [], [], []
    for j in range(2):
        lanes = slice(j * HD, (j + 1) * HD)
        weights = w_ref[j]
        probs = weights.astype(f32)
        grad = g_ref[:, lanes]
        grad_weights = contract_cols(grad, v_ref[:, lanes])
        delta = jnp.sum(probs * grad_weights, axis=-1, keepdims=True)
        grad_scores = (probs * (grad_weights - delta)).astype(bf16)
        dqs.append((matmul(grad_scores, k_ref[:, lanes]) * (HD**-0.5)).astype(bf16))
        dks.append((contract_rows(grad_scores, q_ref[:, lanes]) * (HD**-0.5)).astype(bf16))
        dvs.append(contract_rows(weights, grad).astype(bf16))
    dq_ref[...] = jnp.concatenate(dqs, axis=1)
    dk_ref[...] = jnp.concatenate(dks, axis=1)
    dv_ref[...] = jnp.concatenate(dvs, axis=1)


def attend_forward(queries, keys, values, info, half):
    rows, width = queries.shape
    total = keys.shape[0]
    pairs = width // (4 * HD)
    width = width // 2
    skip = half * pairs
    small = pl.BlockSpec((rows, 2 * HD), lambda h, s: (0, h))
    part = pl.BlockSpec((rows, 2 * HD), lambda h, s: (0, skip + h))
    large = pl.BlockSpec((total, 2 * HD), lambda h, s: (0, skip + h))
    return pl.pallas_call(
        forward_kernel,
        grid_spec=pltpu.PrefetchScalarGridSpec(
            num_scalar_prefetch=1,
            grid=(pairs,),
            in_specs=[part, large, large],
            out_specs=[small, pl.BlockSpec((2, rows, total), lambda h, s: (h, 0, 0))],
            scratch_shapes=[pltpu.VMEM((rows, total), f32)],
        ),
        out_shape=[
            jax.ShapeDtypeStruct((rows, width), bf16),
            jax.ShapeDtypeStruct((2 * pairs, rows, total), bf16),
        ],
        name="attend_forward",
    )(info, queries, keys, values)


def attend_backward(queries, keys, values, grad, weights, half):
    rows, width = queries.shape
    total = keys.shape[0]
    pairs = width // (4 * HD)
    width = width // 2
    skip = half * pairs
    small = pl.BlockSpec((rows, 2 * HD), lambda h: (0, h))
    large = pl.BlockSpec((total, 2 * HD), lambda h: (0, h))
    part = pl.BlockSpec((rows, 2 * HD), lambda h: (0, skip + h))
    deep = pl.BlockSpec((total, 2 * HD), lambda h: (0, skip + h))
    return pl.pallas_call(
        backward_kernel,
        grid=(pairs,),
        in_specs=[part, deep, deep, part, pl.BlockSpec((2, rows, total), lambda h: (h, 0, 0))],
        out_specs=[small, large, large],
        out_shape=[
            jax.ShapeDtypeStruct((rows, width), bf16),
            jax.ShapeDtypeStruct((total, width), bf16),
            jax.ShapeDtypeStruct((total, width), bf16),
        ],
        name="attend_backward",
    )(queries, keys, values, grad, weights)


def feed_kernel(with_start, with_send, *refs):
    x_ref, g_ref, w_ref = refs[:3]
    starts = refs[3:5] if with_start else ()
    dh_ref, act_ref, out_ref, dx_ref = refs[3 + len(starts) : 7 + len(starts)]
    pad = act_ref.shape[2]
    weights = w_ref[0]
    gate_up = weights[:, : 2 * pad]
    down_t = weights[:, 2 * pad :]
    hidden = matmul(x_ref[...], gate_up)
    gate, up = hidden[:, :pad], hidden[:, pad:]
    sigmoid = jax.nn.sigmoid(gate)
    silu = gate * sigmoid
    act = (silu * up).astype(bf16)
    act_ref[0] = act
    grad_act = matmul(g_ref[...], down_t)
    grad_gate = (grad_act * up * sigmoid * (1.0 + gate * (1.0 - sigmoid))).astype(bf16)
    grad_up = (grad_act * silu).astype(bf16)
    grad_hidden = jnp.concatenate([grad_gate, grad_up], axis=1)
    dh_ref[0] = grad_hidden

    @pl.when(pl.program_id(0) == 0)
    def _():
        if with_start:
            out_ref[...] = starts[0][...]
            dx_ref[...] = starts[1][...]
        else:
            out_ref[...] = jnp.zeros_like(out_ref)
            dx_ref[...] = jnp.zeros_like(dx_ref)

    out_ref[...] += contract_cols(act, down_t)
    dx_ref[...] += contract_cols(grad_hidden, gate_up)
    if not with_start:

        @pl.when(pl.program_id(0) == 0)
        def _():
            refs[-2][...] = x_ref[...].T
            refs[-1][...] = g_ref[...].T

    if with_send:

        @pl.when(pl.program_id(0) == pl.num_programs(0) - 1)
        def _():
            half = out_ref.shape[0] // 2
            refs[-2][...] = out_ref[half:, :].astype(bf16)
            refs[-1][...] = dx_ref[half:, :].astype(bf16)


def feed_forward(both_two, both_up, weights, starts=(), with_send=False):
    count, model, lanes = weights.shape
    rows = both_two.shape[0]
    pad = lanes // 3
    whole = pl.BlockSpec((rows, model), lambda k: (0, 0))
    extra = (rows // 2, model) if with_send else (model, rows)
    return pl.pallas_call(
        functools.partial(feed_kernel, len(starts) > 0, with_send),
        grid=(count,),
        in_specs=[whole, whole, pl.BlockSpec((1, model, lanes), lambda k: (k, 0, 0))] + [whole] * len(starts),
        out_specs=[
            pl.BlockSpec((1, rows, 2 * pad), lambda k: (k, 0, 0)),
            pl.BlockSpec((1, rows, pad), lambda k: (k, 0, 0)),
            whole,
            whole,
        ]
        + [pl.BlockSpec(extra, lambda k: (0, 0))] * 2,
        out_shape=[
            jax.ShapeDtypeStruct((count, rows, 2 * pad), bf16),
            jax.ShapeDtypeStruct((count, rows, pad), bf16),
            jax.ShapeDtypeStruct((rows, model), f32),
            jax.ShapeDtypeStruct((rows, model), f32),
        ]
        + [jax.ShapeDtypeStruct(extra, bf16)] * 2,
        name="feed_forward",
    )(both_two, both_up, weights, *starts)


def feed_grad_kernel(spots, *refs):
    dh_ref, act_ref, a_ref, b_ref = refs[8:]
    pad = act_ref.shape[2]
    half = a_ref.shape[1]
    left = jnp.concatenate([ref[...] for ref in refs[:4]], axis=0)
    both = matmul(left, dh_ref[0]).astype(bf16)
    a_ref[0, :, : 2 * pad] = both[:half]
    b_ref[0, :, : 2 * pad] = both[half:]
    left = jnp.concatenate([ref[...] for ref in refs[4:8]], axis=0)
    both = matmul(left, act_ref[0]).astype(bf16)
    a_ref[0, :, 2 * pad :] = both[:half]
    b_ref[0, :, 2 * pad :] = both[half:]


def feed_grads(spots, two_turned, up_turned, grad_hidden, act):
    model, rows = two_turned.shape
    count, _, pad = act.shape
    block = model // 8
    spot_specs = [pl.BlockSpec((block, rows), functools.partial(lambda i, k, s: (s[i], 0), i)) for i in range(4)]
    out = pl.BlockSpec((1, 2 * block, 3 * pad), lambda k, s: (k, 0, 0))
    return pl.pallas_call(
        feed_grad_kernel,
        grid_spec=pltpu.PrefetchScalarGridSpec(
            num_scalar_prefetch=1,
            grid=(count,),
            in_specs=spot_specs
            + spot_specs
            + [
                pl.BlockSpec((1, rows, 2 * pad), lambda k, s: (k, 0, 0)),
                pl.BlockSpec((1, rows, pad), lambda k, s: (k, 0, 0)),
            ],
            out_specs=[out, out],
        ),
        out_shape=[jax.ShapeDtypeStruct((count, 2 * block, 3 * pad), bf16)] * 2,
        name="feed_grads",
    )(spots, *([two_turned] * 4), *([up_turned] * 4), grad_hidden, act)


def tie(*arrays):
    return lax.optimization_barrier(arrays)


def local(
    tokens,
    cotangent,
    seq_lengths,
    attention_gain,
    query_weight,
    latent_down,
    key_up,
    value_up,
    out_weight,
    feedforward_gain,
    gate_weight,
    up_weight,
    down_weight,
):
    tp = lax.axis_index("tp")
    dp = lax.axis_index("dp")
    planes = lax.axis_size("tp")
    dp_count = lax.axis_size("dp")
    dp_bits = dp_count.bit_length() - 1
    core, xbit, ybit = (dp & 1, (dp >> 1) & 1, (dp >> 2) & 1)
    eighth = dp & 7
    rows, model = tokens.shape
    lat_width, quarter = key_up.shape
    width = planes * quarter
    high = dp_count // 8
    part = model // dp_count
    block = model // 8
    up_part = lat_width // dp_count
    plane_of = [(tp + planes - k) % planes for k in range(planes)]
    boundary = seq_lengths[0, 0]

    def ring_gather(piece):
        got = [piece]
        for _ in range(1, planes):
            got.append(ring(got[-1], 1))
        return got

    def blocks_first(array):
        if high == 1:
            return array
        shaped = array.reshape(array.shape[0], high, 8, part)
        return shaped.transpose(0, 2, 1, 3).reshape(array.shape)

    q_piece = lax.dynamic_slice_in_dim(query_weight, eighth * block, block, 0)

    inputs = tokens.astype(f32)
    normed_one, factor_one = normalize(inputs)
    rows_one = (normed_one * attention_gain).astype(bf16)
    latent_own = matmul(rows_one, latent_down).astype(bf16)
    up_piece = jnp.where(core == 0, key_up, value_up)
    o_piece = lax.dynamic_slice_in_dim(out_weight, eighth * block, block, 1)
    lat_up = jnp.concatenate([latent_own, up_piece, o_piece], axis=1)
    q_list, lat_got = [q_piece], [lat_up]
    q_list.append(ring(q_piece, 1))
    lat_got.append(ring(lat_up, 1))
    q_list.append(ring(q_list[1], 1))
    q_next, lat_next = tie(q_list[2], lat_got[1])
    q_list.append(ring(q_next, 1))
    lat_got.append(ring(lat_next, 1))
    q_all = gather_bits(jnp.stack(q_list), (1,), dp)
    q_all, lat_next = tie(q_all, lat_got[2])
    q_all = gather_bits(q_all, (2, 0), dp)
    lat_got.append(ring(lat_next, 1))
    latents = jnp.concatenate([got[:, : 2 * lat_width] for got in lat_got], axis=0)
    up_mine = jnp.concatenate([got[:, 2 * lat_width : 2 * lat_width + quarter] for got in lat_got], axis=1)
    up_other = swap(up_mine, "dp", 0)
    keys_up = jnp.where(core == 0, up_mine, up_other)
    values_up = jnp.where(core == 0, up_other, up_mine)
    groups = [plane_of[k] * 2 // planes for k in range(planes)]
    group_row = jnp.concatenate(
        [jnp.full((1, quarter), 1, jnp.int32) * groups[k].astype(jnp.int32) for k in range(planes)], axis=1
    )

    def both_groups(array):
        zero = jnp.zeros_like(array)
        return jnp.concatenate([jnp.where(group_row == g, array, zero) for g in range(2)], axis=0)

    keys_wide, values_wide = both_groups(keys_up), both_groups(values_up)

    query_full = q_all.transpose(1, 2, 0, 4, 3, 5).reshape(model, width)

    gate_weight, _ = tie(gate_weight, q_list[1])
    up_weight, _ = tie(up_weight, q_list[3])
    down_weight, _ = tie(down_weight, lat_got[2])
    ff_half = gate_weight.shape[1] // 2
    ff_pad = -(-ff_half // 128) * 128

    def core_half(array):
        chosen = jnp.where(core == 0, array[:, :ff_half], array[:, ff_half:])
        return jnp.pad(chosen, ((0, 0), (0, ff_pad - ff_half)))

    down_half = lax.dynamic_slice_in_dim(down_weight, core * ff_half, ff_half, 0)
    down_turned = jnp.pad(down_half.T, ((0, 0), (0, ff_pad - ff_half)))
    ff_own = jnp.concatenate([core_half(gate_weight), core_half(up_weight), down_turned], axis=1)
    spot = (dp >> 1) & 3
    turned_spot = xbit * 2 + ybit
    ff_a = lax.dynamic_slice_in_dim(ff_own, spot * block, block, 0)
    ff_b = lax.dynamic_slice_in_dim(ff_own, model // 2 + turned_spot * block, block, 0)
    ff_piece, _ = tie(jnp.concatenate([ff_a, ff_b], axis=0), lat_got[planes - 1])
    ff_pieces = ring_gather(ff_piece)
    ff_weights = [ff_own]
    for k in range(1, planes):
        top = gather_bits(ff_pieces[k][:block], (1, 2), dp).reshape(model // 2, 3 * ff_pad)
        bottom = gather_bits(ff_pieces[k][block:], (2, 1), dp).reshape(model // 2, 3 * ff_pad)
        ff_weights.append(jnp.concatenate([top, bottom], axis=0))
    cut = planes // 2
    ff_early, ff_late = jnp.stack(ff_weights[:cut]), jnp.stack(ff_weights[cut:])

    o_got = jnp.concatenate([got[:, 2 * lat_width + quarter :] for got in lat_got], axis=0)
    o_got = gather_bits(o_got, (1, 2, 0), dp)
    out_full = o_got.transpose(3, 1, 2, 0, 4).reshape(width, model)

    queries = matmul(rows_one, query_full).astype(bf16)
    keys = matmul(latents, keys_wide).astype(bf16)
    values = matmul(latents, values_wide).astype(bf16)
    queries, out_full = tie(queries, out_full)
    info = jnp.stack([boundary] + [plane_of[k].astype(jnp.int32) * rows for k in range(planes)])
    attended, weights = [], []
    for half in range(2):
        got, kept_weights = attend_forward(queries, keys, values, info, half)
        attended.append(got)
        weights.append(kept_weights)
    attended = jnp.concatenate(attended, axis=1)
    mixed = inputs + matmul(attended, out_full)
    normed_two, factor_two = normalize(mixed)
    rows_two = (normed_two * feedforward_gain).astype(bf16)

    both_two = jnp.concatenate([rows_two, swap(rows_two, "dp", 0)], axis=0)
    both_up = jnp.concatenate([cotangent, swap(cotangent, "dp", 0)], axis=0)

    def rows_first(array):
        if high == 1:
            return array
        shaped = array.reshape(high, 8, part, array.shape[1])
        return shaped.transpose(1, 0, 2, 3).reshape(array.shape)

    def ff_blocks(which, grads):
        spots = jnp.stack([eighth ^ b for b in which]).astype(jnp.int32)
        return feed_grads(spots, *lefts, *grads)

    sent = (2, 6, 5, 7)
    kept = (0, 4, 1, 3)

    def high_bits(array):
        for bit in range(dp_bits - 1, 2, -1):
            array = array.reshape((2, -1) + array.shape[1:])
            array = halve(array, bit, 0, dp)
        return array.reshape(array.shape[1:])

    def finish(side_a, side_b):
        if high > 1:
            count = side_a.shape[0]
            both = jnp.stack([side_a, side_b], axis=2).reshape(count, high, part, 2, 3 * ff_pad)
            both = high_bits(both.transpose(1, 2, 0, 3, 4))
            side_a, side_b = both[:, :, 0].transpose(1, 0, 2), both[:, :, 1].transpose(1, 0, 2)
        return [jnp.stack([side_a[k], side_b[k]]) for k in range(side_a.shape[0])]

    *early_grads, out_sum, grad_sum, two_turned, up_turned = feed_forward(both_two, both_up, ff_early)
    lefts = (rows_first(two_turned), rows_first(up_turned))
    send_a, send_b = ff_blocks(sent, early_grads)
    send_a, send_b, ff_late = tie(send_a, send_b, ff_late)
    early_a, early_b = swap(send_a, "dp", 1), swap(send_b, "dp", 2)
    *late_grads, out_sum, grad_sum, out_send, grad_send = feed_forward(
        both_two, both_up, ff_late, (out_sum, grad_sum), True
    )
    grad_two = grad_sum[:rows] + swap(grad_send, "dp", 0).astype(f32)
    send_a, send_b = ff_blocks(sent, late_grads)
    late_a, late_b = swap(send_a, "dp", 1), swap(send_b, "dp", 2)
    back_two, gain_two = norm_backward(grad_two, normed_two, factor_two, feedforward_gain)
    grad_mixed = cotangent.astype(f32) + back_two
    output = (mixed + out_sum[:rows] + swap(out_send, "dp", 0).astype(f32)).astype(bf16)

    near = (0, 4, 2, 6)
    far = (1, 5, 3, 7)

    def columns(array, blocks):
        array = blocks_first(array)
        return jnp.concatenate(
            [lax.dynamic_slice_in_dim(array, (eighth ^ b) * block, block, 1) for b in blocks], axis=1
        )

    def block_rows(array, blocks):
        shaped = array.reshape(high, 8, up_part, array.shape[1])
        return jnp.stack(
            [pick(shaped, eighth ^ b, 1).reshape(high * up_part, array.shape[1]) for b in blocks]
        )

    def plane_sum(take):
        parts = [take(r) for r in range(planes)]
        bit = planes.bit_length() - 2
        while len(parts) > 1:
            half = len(parts) // 2
            got = swap(jnp.concatenate([p.astype(bf16) for p in parts[half:]], axis=1), "tp", bit)
            size = parts[0].shape[1]
            parts = [parts[i].astype(f32) + got[:, i * size : (i + 1) * size].astype(f32) for i in range(half)]
            bit -= 1
        return parts[0]

    def ring_columns(array):
        return lambda r: lax.dynamic_slice_in_dim(
            array, ((tp - (tp ^ r) + planes) % planes) * quarter, quarter, 1
        )

    mixed_rows = grad_mixed.astype(bf16)
    grad_attended = contract_cols(mixed_rows, out_full).astype(bf16)
    out_part = contract_rows(mixed_rows, attended).astype(bf16)
    out_part = lax.psum_scatter(out_part, "dp", scatter_dimension=0, tiled=True)

    grad_attended, _, _ = tie(grad_attended, send_a, send_b)

    def back(half, grad):
        return attend_backward(queries, keys, values, grad, weights[half], half)

    def kept_blocks(grads):
        return ff_blocks(kept, grads)

    first_back = back(0, grad_attended)
    early_hidden, early_act, first_query = tie(*early_grads, first_back[0])
    keep_a, keep_b = kept_blocks((early_hidden, early_act))
    next_a = rounded_sum(keep_a[:, block:], early_a[:, block:])
    next_b = rounded_sum(keep_b[:, block:], early_b[:, block:])
    grad_attended, next_a, next_b = tie(grad_attended, next_a, next_b)
    early_next_a, early_next_b = swap(next_a, "dp", 2), swap(next_b, "dp", 1)
    own_a = rounded_sum(keep_a[:, :block], early_a[:, :block])
    own_b = rounded_sum(keep_b[:, :block], early_b[:, :block])
    second_back = back(1, grad_attended)
    grad_queries, grad_keys, grad_values = [
        jnp.concatenate(pair, axis=1) for pair in zip((first_query, *first_back[1:]), second_back)
    ]
    latent_part = (contract_cols(grad_keys, keys_wide) + contract_cols(grad_values, values_wide)).astype(bf16)
    late_hidden, late_act, latent_part = tie(*late_grads, latent_part)

    def lat_rows(k):
        return latent_part[k * rows : (k + 1) * rows]

    lat_one = ring(lat_rows(3), -1)
    keep_a, keep_b = kept_blocks((late_hidden, late_act))
    next_a = rounded_sum(keep_a[:, block:], late_a[:, block:])
    next_b = rounded_sum(keep_b[:, block:], late_b[:, block:])
    late_queries, next_a, next_b = tie(grad_queries, next_a, next_b)
    late_next_a, late_next_b = swap(next_a, "dp", 2), swap(next_b, "dp", 1)

    def one_group(array):
        return jnp.where(group_row == 0, array[:lat_width], array[lat_width:])

    key_part = one_group(contract_rows(latents, grad_keys)).astype(bf16)
    value_part = one_group(contract_rows(latents, grad_values)).astype(bf16)
    one_near, one_far = columns(rows_one, near), columns(rows_one, far)

    def late(left, blocks):
        of_query = contract_rows(left, late_queries)
        of_query = of_query.astype(bf16).reshape(4, block, width)
        return jnp.concatenate([of_query, block_rows(key_part, blocks), block_rows(value_part, blocks)], axis=1)

    late_got = swap(late(one_far, far), "dp", 0)
    ff_parts = finish(rounded_sum(own_a, early_next_a), rounded_sum(own_b, early_next_b))
    lat_next, ff_next = tie(rounded_sum(lat_one, lat_rows(2)), ff_parts[1])
    lat_two = ring(lat_next, -1)
    ff_next = ring(ff_next, 1)
    late_sum = rounded_sum(late(one_near, near), late_got)
    lat_next, late_sum = tie(rounded_sum(lat_two, lat_rows(1)), late_sum)
    lat_three = ring(lat_next, -1)
    late_got = swap(late_sum[2:], "dp", 1)
    grad_latent = rounded_sum(lat_three, lat_rows(0))
    own_a = rounded_sum(keep_a[:, :block], late_a[:, :block])
    own_b = rounded_sum(keep_b[:, :block], late_b[:, :block])

    grad_one = contract_cols(grad_queries, query_full) + contract_cols(grad_latent, latent_down)
    back_one, gain_one = norm_backward(grad_one, normed_one, factor_one, attention_gain)
    tokens_grad = grad_mixed + back_one

    gains = jnp.stack([gain_one, gain_two])

    def last(left, blocks):
        extra = jnp.pad(columns(gains, blocks).T.astype(bf16), ((0, 0), (0, 126)))
        both = jnp.concatenate([contract_rows(left, grad_latent).astype(bf16), extra], axis=1)
        return both.reshape(4, block, both.shape[1])

    last_sum = rounded_sum(last(one_near, near), swap(last(one_far, far), "dp", 0))
    late_sum = rounded_sum(late_sum[:2], late_got)
    ff_parts += finish(rounded_sum(own_a, late_next_a), rounded_sum(own_b, late_next_b))
    ff_next = rounded_sum(ff_next, ff_parts[2])
    last_sum, ff_next, late_sum, out_part = tie(last_sum, ff_next, late_sum, out_part)
    out_grad = plane_sum(ring_columns(out_part)).T
    ff_next = ring(ff_next, 1)
    last_sum = rounded_sum(last_sum[:2], swap(last_sum[2:], "dp", 1))
    late_sum = rounded_sum(late_sum[0], swap(late_sum[1], "dp", 2))
    last_sum = rounded_sum(last_sum[0], swap(last_sum[1], "dp", 2))
    if high > 1:
        cuts = [late_sum[:block], late_sum[block : block + lat_width // 8], late_sum[block + lat_width // 8 :]]
        late_sum = high_bits(jnp.concatenate([cut.reshape(high, -1, width) for cut in cuts], axis=1))
        last_sum = high_bits(last_sum.reshape(high, part, last_sum.shape[1]))
    ff_next = rounded_sum(ff_next, ff_parts[3])
    last_sum, ff_next, late_sum = tie(last_sum, ff_next, late_sum)
    ff_total = ring(ff_next, 1).astype(f32) + ff_parts[0].astype(f32)
    lat_cols = 2 * lat_width // planes

    def last_columns(r):
        return jnp.concatenate(
            [
                lax.dynamic_slice_in_dim(last_sum, (tp ^ r) * lat_cols, lat_cols, 1),
                last_sum[:, 2 * lat_width :],
            ],
            axis=1,
        )

    rows_last, rows_late = part, part + 2 * up_part
    late_columns = ring_columns(late_sum)
    tail = plane_sum(lambda r: jnp.concatenate([last_columns(r), late_columns(r)], axis=0))
    last_sum = tail[:rows_last]
    late_sum = tail[rows_last : rows_last + rows_late]
    query_grad = late_sum[:part]
    key_grad = late_sum[part : part + up_part]
    value_grad = late_sum[part + up_part :]

    ff_mine = ff_total[0]
    ff_other = swap(ff_total[1], "dp", 0)
    ff_first = jnp.where(core == 0, ff_mine, ff_other)
    ff_second = jnp.where(core == 0, ff_other, ff_mine)

    def joined(index):
        lanes = slice(index * ff_pad, index * ff_pad + ff_half)
        return jnp.concatenate([ff_first[:, lanes], ff_second[:, lanes]], axis=1)

    gate_grad, up_grad, down_grad = joined(0), joined(1), joined(2).T
    latent_grad = last_sum[:, :lat_cols]
    return (
        output,
        tokens_grad,
        last_sum[:, lat_cols],
        query_grad,
        latent_grad,
        key_grad,
        value_grad,
        out_grad,
        last_sum[:, lat_cols + 1],
        gate_grad,
        up_grad,
        down_grad,
    )


def solution(mesh):
    return jax.shard_map(
        local,
        mesh=mesh,
        in_specs=(
            P(("dp", "tp"), None),
            P(("dp", "tp"), None),
            P("dp", None),
            P(),
            P(None, "tp"),
            P(),
            P(None, "tp"),
            P(None, "tp"),
            P("tp", None),
            P(),
            P(None, "tp"),
            P(None, "tp"),
            P("tp", None),
        ),
        out_specs=(
            P(("dp", "tp"), None),
            P(("dp", "tp"), None),
            P("dp"),
            P("dp", "tp"),
            P("dp", "tp"),
            P("dp", "tp"),
            P("dp", "tp"),
            P("tp", "dp"),
            P("dp"),
            P("dp", "tp"),
            P("dp", "tp"),
            P("tp", "dp"),
        ),
        check_vma=False,
    )
```

```python
import functools

import jax
import jax.numpy as jnp
from jax import lax
from jax.experimental import pallas as pl
from jax.experimental.pallas import tpu as pltpu
from jax.sharding import PartitionSpec as P


HD = 64
norm_eps = 1e-06
masked_score = -1000000000.0
bf16 = jnp.bfloat16
f32 = jnp.float32


def matmul(left, right):
    return jnp.dot(left, right, preferred_element_type=f32)


def contract_rows(left, right):
    return lax.dot_general(left, right, (((0,), (0,)), ((), ())), preferred_element_type=f32)


def contract_cols(left, right):
    return lax.dot_general(left, right, (((1,), (1,)), ((), ())), preferred_element_type=f32)


def normalize(values):
    factor = lax.rsqrt(jnp.mean(values * values, axis=-1, keepdims=True) + norm_eps)
    return (values * factor, factor)


def norm_backward(upstream, normed, factor, scaling):
    weighted = scaling * upstream
    inner = jnp.mean(weighted * normed, axis=-1, keepdims=True)
    return (factor * (weighted - normed * inner), jnp.sum(upstream * normed, axis=0))


def swap(block, axis, bit):
    count = lax.axis_size(axis)
    return lax.ppermute(block, axis, [(i, i ^ (1 << bit)) for i in range(count)])


def ring(block, step):
    count = lax.axis_size("tp")
    return lax.ppermute(block, "tp", [(i, (i + step) % count) for i in range(count)])


def pick(block, index, axis):
    return lax.dynamic_index_in_dim(block, index, axis, keepdims=False)


def rounded_sum(left, right):
    return (left.astype(f32) + right.astype(f32)).astype(bf16)


def gather_bits(block, bits, dp):
    for bit in bits:
        mine = (dp >> bit) & 1
        other = swap(block, "dp", bit)
        first = jnp.where(mine == 0, block, other)
        second = jnp.where(mine == 0, other, block)
        block = jnp.stack([first, second])
    return block


def halve(block, bit, axis, dp):
    mine = (dp >> bit) & 1
    keep = pick(block, mine, axis)
    send = pick(block, 1 - mine, axis)
    return rounded_sum(keep, swap(send, "dp", bit))


def forward_kernel(info, q_ref, k_ref, v_ref, *refs):
    o_ref, w_ref, bias_ref = refs[-3:]
    rows, keys = bias_ref.shape

    @pl.when(pl.program_id(0) == 0)
    def _():
        edge = info[0]
        for k in range(keys // rows):
            row = lax.broadcasted_iota(jnp.int32, (rows, rows), 0) + info[1]
            col = lax.broadcasted_iota(jnp.int32, (rows, rows), 1) + info[1 + k]
            same = (col >= edge).astype(jnp.int32) == (row >= edge).astype(jnp.int32)
            bias_ref[:, k * rows : (k + 1) * rows] = jnp.where(same & (col <= row), 0.0, masked_score)

    outs = []
    for j in range(2):
        lanes = slice(j * HD, (j + 1) * HD)
        scores = contract_cols(q_ref[:, lanes], k_ref[:, lanes]) * (HD**-0.5) + bias_ref[...]
        top = jnp.max(scores, axis=-1, keepdims=True)
        shifted = jnp.exp(scores - top)
        total = jnp.sum(shifted, axis=-1, keepdims=True)
        weights = (shifted * (1.0 / total)).astype(bf16)
        w_ref[j] = weights
        outs.append(matmul(weights, v_ref[:, lanes]).astype(bf16))
    o_ref[...] = jnp.concatenate(outs, axis=1)


def backward_kernel(q_ref, k_ref, v_ref, g_ref, w_ref, *refs):
    dq_ref, dk_ref, dv_ref = refs[-3:]
    dqs, dks, dvs = [], [], []
    for j in range(2):
        lanes = slice(j * HD, (j + 1) * HD)
        weights = w_ref[j]
        probs = weights.astype(f32)
        grad = g_ref[:, lanes]
        grad_weights = contract_cols(grad, v_ref[:, lanes])
        delta = jnp.sum(probs * grad_weights, axis=-1, keepdims=True)
        grad_scores = (probs * (grad_weights - delta)).astype(bf16)
        dqs.append((matmul(grad_scores, k_ref[:, lanes]) * (HD**-0.5)).astype(bf16))
        dks.append((contract_rows(grad_scores, q_ref[:, lanes]) * (HD**-0.5)).astype(bf16))
        dvs.append(contract_rows(weights, grad).astype(bf16))
    dq_ref[...] = jnp.concatenate(dqs, axis=1)
    dk_ref[...] = jnp.concatenate(dks, axis=1)
    dv_ref[...] = jnp.concatenate(dvs, axis=1)


def attend_forward(queries, keys, values, info, half, *started):
    rows, width = queries.shape
    total = keys.shape[0]
    pairs = width // (4 * HD)
    skip = half * pairs
    part = pl.BlockSpec((rows, 2 * HD), lambda h, s: (0, skip + h))
    large = pl.BlockSpec((total, 2 * HD), lambda h, s: (0, skip + h))
    return pl.pallas_call(
        forward_kernel,
        grid_spec=pltpu.PrefetchScalarGridSpec(
            num_scalar_prefetch=1,
            grid=(pairs,),
            in_specs=[part, large, large] + [pl.BlockSpec(memory_space=pl.ANY)] * len(started),
            out_specs=[part, pl.BlockSpec((2, rows, total), lambda h, s: (h, 0, 0))],
            scratch_shapes=[pltpu.VMEM((rows, total), f32)],
        ),
        out_shape=[
            jax.ShapeDtypeStruct((rows, width), bf16),
            jax.ShapeDtypeStruct((2 * pairs, rows, total), bf16),
        ],
        input_output_aliases={4: 0} if started else {},
        name="attend_forward",
    )(info, queries, keys, values, *started)


def attend_backward(queries, keys, values, grad, weights, half, *started):
    rows, width = queries.shape
    total = keys.shape[0]
    pairs = width // (4 * HD)
    skip = half * pairs
    part = pl.BlockSpec((rows, 2 * HD), lambda h: (0, skip + h))
    deep = pl.BlockSpec((total, 2 * HD), lambda h: (0, skip + h))
    return pl.pallas_call(
        backward_kernel,
        grid=(pairs,),
        in_specs=[part, deep, deep, part, pl.BlockSpec((2, rows, total), lambda h: (h, 0, 0))]
        + [pl.BlockSpec(memory_space=pl.ANY)] * len(started),
        out_specs=[part, deep, deep],
        out_shape=[
            jax.ShapeDtypeStruct((rows, width), bf16),
            jax.ShapeDtypeStruct((total, width), bf16),
            jax.ShapeDtypeStruct((total, width), bf16),
        ],
        input_output_aliases={5: 0, 6: 1, 7: 2} if started else {},
        name="attend_backward",
    )(queries, keys, values, grad, weights, *started)


def feed_kernel(with_start, with_send, *refs):
    x_ref, g_ref, w_ref = refs[:3]
    starts = refs[3:5] if with_start else ()
    dh_ref, act_ref, out_ref, dx_ref = refs[3 + len(starts) : 7 + len(starts)]
    pad = act_ref.shape[2]
    weights = w_ref[0]
    gate_up = weights[:, : 2 * pad]
    down_t = weights[:, 2 * pad :]
    hidden = matmul(x_ref[...], gate_up)
    gate, up = hidden[:, :pad], hidden[:, pad:]
    sigmoid = jax.nn.sigmoid(gate)
    silu = gate * sigmoid
    act = (silu * up).astype(bf16)
    act_ref[0] = act
    grad_act = matmul(g_ref[...], down_t)
    grad_gate = (grad_act * up * sigmoid * (1.0 + gate * (1.0 - sigmoid))).astype(bf16)
    grad_up = (grad_act * silu).astype(bf16)
    grad_hidden = jnp.concatenate([grad_gate, grad_up], axis=1)
    dh_ref[0] = grad_hidden

    @pl.when(pl.program_id(0) == 0)
    def _():
        if with_start:
            out_ref[...] = starts[0][...]
            dx_ref[...] = starts[1][...]
        else:
            out_ref[...] = jnp.zeros_like(out_ref)
            dx_ref[...] = jnp.zeros_like(dx_ref)

    out_ref[...] += contract_cols(act, down_t)
    dx_ref[...] += contract_cols(grad_hidden, gate_up)
    if not with_start:

        @pl.when(pl.program_id(0) == 0)
        def _():
            refs[-2][...] = x_ref[...].T
            refs[-1][...] = g_ref[...].T

    if with_send:

        @pl.when(pl.program_id(0) == pl.num_programs(0) - 1)
        def _():
            half = out_ref.shape[0] // 2
            refs[-2][...] = out_ref[half:, :].astype(bf16)
            refs[-1][...] = dx_ref[half:, :].astype(bf16)


def feed_forward(both_two, both_up, weights, starts=(), with_send=False):
    count, model, lanes = weights.shape
    rows = both_two.shape[0]
    pad = lanes // 3
    whole = pl.BlockSpec((rows, model), lambda k: (0, 0))
    extra = (rows // 2, model) if with_send else (model, rows)
    return pl.pallas_call(
        functools.partial(feed_kernel, len(starts) > 0, with_send),
        grid=(count,),
        in_specs=[whole, whole, pl.BlockSpec((1, model, lanes), lambda k: (k, 0, 0))] + [whole] * len(starts),
        out_specs=[
            pl.BlockSpec((1, rows, 2 * pad), lambda k: (k, 0, 0)),
            pl.BlockSpec((1, rows, pad), lambda k: (k, 0, 0)),
            whole,
            whole,
        ]
        + [pl.BlockSpec(extra, lambda k: (0, 0))] * 2,
        out_shape=[
            jax.ShapeDtypeStruct((count, rows, 2 * pad), bf16),
            jax.ShapeDtypeStruct((count, rows, pad), bf16),
            jax.ShapeDtypeStruct((rows, model), f32),
            jax.ShapeDtypeStruct((rows, model), f32),
        ]
        + [jax.ShapeDtypeStruct(extra, bf16)] * 2,
        name="feed_forward",
    )(both_two, both_up, weights, *starts)


def feed_grad_kernel(spots, *refs):
    dh_ref, act_ref, a_ref, b_ref = refs[8:]
    pad = act_ref.shape[2]
    half = a_ref.shape[1]
    left = jnp.concatenate([ref[...] for ref in refs[:4]], axis=0)
    both = matmul(left, dh_ref[0]).astype(bf16)
    a_ref[0, :, : 2 * pad] = both[:half]
    b_ref[0, :, : 2 * pad] = both[half:]
    left = jnp.concatenate([ref[...] for ref in refs[4:8]], axis=0)
    both = matmul(left, act_ref[0]).astype(bf16)
    a_ref[0, :, 2 * pad :] = both[:half]
    b_ref[0, :, 2 * pad :] = both[half:]


def feed_grads(spots, two_turned, up_turned, grad_hidden, act):
    model, rows = two_turned.shape
    count, _, pad = act.shape
    block = model // 8
    spot_specs = [pl.BlockSpec((block, rows), functools.partial(lambda i, k, s: (s[i], 0), i)) for i in range(4)]
    out = pl.BlockSpec((1, 2 * block, 3 * pad), lambda k, s: (k, 0, 0))
    return pl.pallas_call(
        feed_grad_kernel,
        grid_spec=pltpu.PrefetchScalarGridSpec(
            num_scalar_prefetch=1,
            grid=(count,),
            in_specs=spot_specs
            + spot_specs
            + [
                pl.BlockSpec((1, rows, 2 * pad), lambda k, s: (k, 0, 0)),
                pl.BlockSpec((1, rows, pad), lambda k, s: (k, 0, 0)),
            ],
            out_specs=[out, out],
        ),
        out_shape=[jax.ShapeDtypeStruct((count, 2 * block, 3 * pad), bf16)] * 2,
        name="feed_grads",
    )(spots, *([two_turned] * 4), *([up_turned] * 4), grad_hidden, act)


def tie(*arrays):
    return lax.optimization_barrier(arrays)


def local(
    tokens,
    cotangent,
    seq_lengths,
    attention_gain,
    query_weight,
    latent_down,
    key_up,
    value_up,
    out_weight,
    feedforward_gain,
    gate_weight,
    up_weight,
    down_weight,
):
    tp = lax.axis_index("tp")
    dp = lax.axis_index("dp")
    planes = lax.axis_size("tp")
    dp_count = lax.axis_size("dp")
    dp_bits = dp_count.bit_length() - 1
    core, xbit, ybit = (dp & 1, (dp >> 1) & 1, (dp >> 2) & 1)
    eighth = dp & 7
    rows, model = tokens.shape
    lat_width, quarter = key_up.shape
    width = planes * quarter
    high = dp_count // 8
    part = model // dp_count
    block = model // 8
    up_part = lat_width // dp_count
    plane_of = [(tp + planes - k) % planes for k in range(planes)]
    boundary = seq_lengths[0, 0]

    def ring_gather(piece):
        got = [piece]
        for _ in range(1, planes):
            got.append(ring(got[-1], 1))
        return got

    def blocks_first(array):
        if high == 1:
            return array
        shaped = array.reshape(array.shape[0], high, 8, part)
        return shaped.transpose(0, 2, 1, 3).reshape(array.shape)

    q_piece = lax.dynamic_slice_in_dim(query_weight, eighth * block, block, 0)

    inputs = tokens.astype(f32)
    normed_one, factor_one = normalize(inputs)
    rows_one = (normed_one * attention_gain).astype(bf16)
    latent_own = matmul(rows_one, latent_down).astype(bf16)
    up_piece = jnp.where(core == 0, key_up, value_up)
    o_piece = lax.dynamic_slice_in_dim(out_weight, eighth * block, block, 1)
    q_turned = jnp.concatenate([q_piece[:, : quarter // 2], q_piece[:, quarter // 2 :]], axis=0)
    lat_up = jnp.concatenate([latent_own, up_piece, o_piece, q_turned], axis=1)
    lat_got = ring_gather(lat_up)
    o_start = 2 * lat_width + quarter
    q_start = o_start + block
    q_all = jnp.stack(
        [jnp.concatenate([got[:block, q_start:], got[block:, q_start:]], axis=1) for got in lat_got]
    )
    q_all = gather_bits(q_all, (1,), dp)
    o_got = jnp.concatenate([got[:, o_start:q_start] for got in lat_got], axis=0)
    q_all, o_got = tie(q_all, o_got)
    q_all = gather_bits(q_all, (2, 0), dp)
    latents = jnp.concatenate([got[:, : 2 * lat_width] for got in lat_got], axis=0)
    up_mine = jnp.concatenate([got[:, 2 * lat_width : 2 * lat_width + quarter] for got in lat_got], axis=1)
    up_other = swap(up_mine, "dp", 0)
    keys_up = jnp.where(core == 0, up_mine, up_other)
    values_up = jnp.where(core == 0, up_other, up_mine)
    groups = [plane_of[k] * 2 // planes for k in range(planes)]
    group_row = jnp.concatenate(
        [jnp.full((1, quarter), 1, jnp.int32) * groups[k].astype(jnp.int32) for k in range(planes)], axis=1
    )

    def both_groups(array):
        zero = jnp.zeros_like(array)
        return jnp.concatenate([jnp.where(group_row == g, array, zero) for g in range(2)], axis=0)

    keys_wide, values_wide = both_groups(keys_up), both_groups(values_up)

    query_full = q_all.transpose(1, 2, 0, 4, 3, 5).reshape(model, width)

    gate_weight, _ = tie(gate_weight, lat_got[1])
    up_weight, _ = tie(up_weight, lat_got[1])
    down_weight, _ = tie(down_weight, lat_got[2])
    ff_half = gate_weight.shape[1] // 2
    ff_pad = -(-ff_half // 128) * 128

    def core_half(array):
        chosen = jnp.where(core == 0, array[:, :ff_half], array[:, ff_half:])
        return jnp.pad(chosen, ((0, 0), (0, ff_pad - ff_half)))

    gate_half, up_half = core_half(gate_weight), core_half(up_weight)
    down_half = lax.dynamic_slice_in_dim(down_weight, core * ff_half, ff_half, 0)
    down_turned = jnp.pad(down_half.T, ((0, 0), (0, ff_pad - ff_half)))
    ff_own = jnp.concatenate([gate_half, up_half, down_turned], axis=1)
    spot = (dp >> 1) & 3
    turned_spot = xbit * 2 + ybit
    ff_a = lax.dynamic_slice_in_dim(ff_own, spot * block, block, 0)
    ff_b = lax.dynamic_slice_in_dim(ff_own, model // 2 + turned_spot * block, block, 0)
    ff_piece, _ = tie(jnp.concatenate([ff_a, ff_b], axis=0), lat_got[planes - 1])
    ff_pieces = ring_gather(ff_piece)
    ff_weights = [ff_own]
    for k in range(1, planes):
        top = gather_bits(ff_pieces[k][:block], (1, 2), dp).reshape(model // 2, 3 * ff_pad)
        bottom = gather_bits(ff_pieces[k][block:], (2, 1), dp).reshape(model // 2, 3 * ff_pad)
        ff_weights.append(jnp.concatenate([top, bottom], axis=0))
    cut = planes // 2
    ff_early, ff_late = jnp.stack(ff_weights[:cut]), jnp.stack(ff_weights[cut:])

    o_got = gather_bits(o_got, (1, 2, 0), dp)
    out_full = o_got.transpose(3, 1, 2, 0, 4).reshape(width, model)

    queries = matmul(rows_one, query_full).astype(bf16)
    keys = matmul(latents, keys_wide).astype(bf16)
    values = matmul(latents, values_wide).astype(bf16)
    info = jnp.stack([boundary] + [plane_of[k].astype(jnp.int32) * rows for k in range(planes)])
    attended, first_weights = attend_forward(queries, keys, values, info, 0)
    attended, out_full = tie(attended, out_full)
    attended, second_weights = attend_forward(queries, keys, values, info, 1, attended)
    weights = (first_weights, second_weights)
    mixed = inputs + matmul(attended, out_full)
    normed_two, factor_two = normalize(mixed)
    rows_two = (normed_two * feedforward_gain).astype(bf16)

    both_two = jnp.concatenate([rows_two, swap(rows_two, "dp", 0)], axis=0)
    both_up = jnp.concatenate([cotangent, swap(cotangent, "dp", 0)], axis=0)

    def rows_first(array):
        if high == 1:
            return array
        shaped = array.reshape(high, 8, part, array.shape[1])
        return shaped.transpose(1, 0, 2, 3).reshape(array.shape)

    def ff_blocks(which, grads):
        spots = jnp.stack([eighth ^ b for b in which]).astype(jnp.int32)
        return feed_grads(spots, *lefts, *grads)

    sent = (2, 6, 5, 7)
    kept = (0, 4, 1, 3)

    def high_bits(array):
        for bit in range(dp_bits - 1, 2, -1):
            array = array.reshape((2, -1) + array.shape[1:])
            array = halve(array, bit, 0, dp)
        return array.reshape(array.shape[1:])

    def finish(side_a, side_b):
        if high > 1:
            count = side_a.shape[0]
            both = jnp.stack([side_a, side_b], axis=2).reshape(count, high, part, 2, 3 * ff_pad)
            both = high_bits(both.transpose(1, 2, 0, 3, 4))
            side_a, side_b = both[:, :, 0].transpose(1, 0, 2), both[:, :, 1].transpose(1, 0, 2)
        return [jnp.stack([side_a[k], side_b[k]]) for k in range(side_a.shape[0])]

    *early_grads, out_sum, grad_sum, two_turned, up_turned = feed_forward(both_two, both_up, ff_early)
    lefts = (rows_first(two_turned), rows_first(up_turned))
    send_a, send_b = ff_blocks(sent, early_grads)
    send_a, send_b, ff_late = tie(send_a, send_b, ff_late)
    early_a, early_b = swap(send_a, "dp", 1), swap(send_b, "dp", 2)
    *late_grads, out_sum, grad_sum, out_send, grad_send = feed_forward(
        both_two, both_up, ff_late, (out_sum, grad_sum), True
    )
    grad_two = grad_sum[:rows] + swap(grad_send, "dp", 0).astype(f32)
    send_a, send_b = ff_blocks(sent, late_grads)
    late_a, late_b = swap(send_a, "dp", 1), swap(send_b, "dp", 2)
    back_two, gain_two = norm_backward(grad_two, normed_two, factor_two, feedforward_gain)
    grad_mixed = cotangent.astype(f32) + back_two
    output = (mixed + out_sum[:rows] + swap(out_send, "dp", 0).astype(f32)).astype(bf16)

    near = (0, 4, 2, 6)
    far = (1, 5, 3, 7)

    def columns(array, blocks):
        array = blocks_first(array)
        return jnp.concatenate(
            [lax.dynamic_slice_in_dim(array, (eighth ^ b) * block, block, 1) for b in blocks], axis=1
        )

    def block_rows(array, blocks):
        shaped = array.reshape(high, 8, up_part, array.shape[1])
        return jnp.stack(
            [pick(shaped, eighth ^ b, 1).reshape(high * up_part, array.shape[1]) for b in blocks]
        )

    def plane_sum(take):
        parts = [take(r) for r in range(planes)]
        bit = planes.bit_length() - 2
        while len(parts) > 1:
            half = len(parts) // 2
            got = swap(jnp.concatenate([p.astype(bf16) for p in parts[half:]], axis=1), "tp", bit)
            size = parts[0].shape[1]
            parts = [parts[i].astype(f32) + got[:, i * size : (i + 1) * size].astype(f32) for i in range(half)]
            bit -= 1
        return parts[0]

    def ring_columns(array):
        return lambda r: lax.dynamic_slice_in_dim(
            array, ((tp - (tp ^ r) + planes) % planes) * quarter, quarter, 1
        )

    mixed_rows = grad_mixed.astype(bf16)
    grad_attended = contract_cols(mixed_rows, out_full).astype(bf16)
    out_part = contract_rows(mixed_rows, attended).astype(bf16)
    out_part = lax.psum_scatter(out_part, "dp", scatter_dimension=0, tiled=True)

    grad_attended, _, _ = tie(grad_attended, send_a, send_b)

    def back(half, grad, *started):
        return attend_backward(queries, keys, values, grad, weights[half], half, *started)

    def kept_blocks(grads):
        return ff_blocks(kept, grads)

    first_back = back(0, grad_attended)
    early_hidden, early_act, first_query = tie(*early_grads, first_back[0])
    keep_a, keep_b = kept_blocks((early_hidden, early_act))
    next_a = rounded_sum(keep_a[:, block:], early_a[:, block:])
    next_b = rounded_sum(keep_b[:, block:], early_b[:, block:])
    grad_attended, next_a, next_b = tie(grad_attended, next_a, next_b)
    early_next_a, early_next_b = swap(next_a, "dp", 2), swap(next_b, "dp", 1)
    own_a = rounded_sum(keep_a[:, :block], early_a[:, :block])
    own_b = rounded_sum(keep_b[:, :block], early_b[:, :block])
    grad_queries, grad_keys, grad_values = back(1, grad_attended, first_query, *first_back[1:])
    latent_part = (contract_cols(grad_keys, keys_wide) + contract_cols(grad_values, values_wide)).astype(bf16)
    late_hidden, late_act, latent_part = tie(*late_grads, latent_part)

    def lat_rows(k):
        return latent_part[k * rows : (k + 1) * rows]

    lat_one = ring(lat_rows(3), -1)
    keep_a, keep_b = kept_blocks((late_hidden, late_act))
    next_a = rounded_sum(keep_a[:, block:], late_a[:, block:])
    next_b = rounded_sum(keep_b[:, block:], late_b[:, block:])
    late_queries, next_a, next_b = tie(grad_queries, next_a, next_b)
    late_next_a, late_next_b = swap(next_a, "dp", 2), swap(next_b, "dp", 1)

    def one_group(array):
        return jnp.where(group_row == 0, array[:lat_width], array[lat_width:])

    key_part = one_group(contract_rows(latents, grad_keys)).astype(bf16)
    value_part = one_group(contract_rows(latents, grad_values)).astype(bf16)
    one_near, one_far = columns(rows_one, near), columns(rows_one, far)

    def late(left, blocks):
        of_query = contract_rows(left, late_queries)
        of_query = of_query.astype(bf16).reshape(4, block, width)
        return jnp.concatenate([of_query, block_rows(key_part, blocks), block_rows(value_part, blocks)], axis=1)

    late_got = swap(late(one_far, far), "dp", 0)
    ff_parts = finish(rounded_sum(own_a, early_next_a), rounded_sum(own_b, early_next_b))
    late_sum = rounded_sum(late(one_near, near), late_got)
    lat_next, ff_next = tie(rounded_sum(lat_one, lat_rows(2)), ff_parts[1])
    lat_two = ring(lat_next, -1)
    ff_next = ring(ff_next, 1)
    lat_two, late_sum, out_part = tie(lat_two, late_sum, out_part)
    out_grad = plane_sum(ring_columns(out_part)).T
    late_got = swap(late_sum[2:], "dp", 1)
    lat_three = ring(rounded_sum(lat_two, lat_rows(1)), -1)
    own_a = rounded_sum(keep_a[:, :block], late_a[:, :block])
    own_b = rounded_sum(keep_b[:, :block], late_b[:, :block])

    ff_parts += finish(rounded_sum(own_a, late_next_a), rounded_sum(own_b, late_next_b))
    grad_latent, ff_next = tie(rounded_sum(lat_three, lat_rows(0)), rounded_sum(ff_next, ff_parts[2]))
    ff_next = ring(ff_next, 1)
    grad_one = contract_cols(grad_queries, query_full) + contract_cols(grad_latent, latent_down)
    back_one, gain_one = norm_backward(grad_one, normed_one, factor_one, attention_gain)
    tokens_grad = grad_mixed + back_one

    gains = jnp.stack([gain_one, gain_two])

    def last(left, blocks):
        extra = jnp.pad(columns(gains, blocks).T.astype(bf16), ((0, 0), (0, 126)))
        both = jnp.concatenate([contract_rows(left, grad_latent).astype(bf16), extra], axis=1)
        return both.reshape(4, block, both.shape[1])

    last_sum = rounded_sum(last(one_near, near), swap(last(one_far, far), "dp", 0))
    late_sum = rounded_sum(late_sum[:2], late_got)
    last_sum, late_sum = tie(last_sum, late_sum)
    last_sum = rounded_sum(last_sum[:2], swap(last_sum[2:], "dp", 1))
    late_sum = rounded_sum(late_sum[0], swap(late_sum[1], "dp", 2))
    last_sum, ff_next = tie(last_sum, rounded_sum(ff_next, ff_parts[3]))
    ff_total = ring(ff_next, 1).astype(f32) + ff_parts[0].astype(f32)
    last_sum = rounded_sum(last_sum[0], swap(last_sum[1], "dp", 2))
    if high > 1:
        cuts = [late_sum[:block], late_sum[block : block + lat_width // 8], late_sum[block + lat_width // 8 :]]
        late_sum = high_bits(jnp.concatenate([cut.reshape(high, -1, width) for cut in cuts], axis=1))
        last_sum = high_bits(last_sum.reshape(high, part, last_sum.shape[1]))
    lat_cols = 2 * lat_width // planes

    def last_columns(r):
        return jnp.concatenate(
            [
                lax.dynamic_slice_in_dim(last_sum, (tp ^ r) * lat_cols, lat_cols, 1),
                last_sum[:, 2 * lat_width :],
            ],
            axis=1,
        )

    rows_last, rows_late = part, part + 2 * up_part
    late_columns = ring_columns(late_sum)
    tail = plane_sum(lambda r: jnp.concatenate([last_columns(r), late_columns(r)], axis=0))
    last_sum = tail[:rows_last]
    late_sum = tail[rows_last : rows_last + rows_late]
    query_grad = late_sum[:part]
    key_grad = late_sum[part : part + up_part]
    value_grad = late_sum[part + up_part :]

    ff_mine = ff_total[0]
    ff_other = swap(ff_total[1], "dp", 0)
    ff_first = jnp.where(core == 0, ff_mine, ff_other)
    ff_second = jnp.where(core == 0, ff_other, ff_mine)

    def joined(index):
        lanes = slice(index * ff_pad, index * ff_pad + ff_half)
        return jnp.concatenate([ff_first[:, lanes], ff_second[:, lanes]], axis=1)

    gate_grad, up_grad, down_grad = joined(0), joined(1), joined(2).T
    latent_grad = last_sum[:, :lat_cols]
    return (
        output,
        tokens_grad,
        last_sum[:, lat_cols],
        query_grad,
        latent_grad,
        key_grad,
        value_grad,
        out_grad,
        last_sum[:, lat_cols + 1],
        gate_grad,
        up_grad,
        down_grad,
    )


def solution(mesh):
    return jax.shard_map(
        local,
        mesh=mesh,
        in_specs=(
            P(("dp", "tp"), None),
            P(("dp", "tp"), None),
            P("dp", None),
            P(),
            P(None, "tp"),
            P(),
            P(None, "tp"),
            P(None, "tp"),
            P("tp", None),
            P(),
            P(None, "tp"),
            P(None, "tp"),
            P("tp", None),
        ),
        out_specs=(
            P(("dp", "tp"), None),
            P(("dp", "tp"), None),
            P("dp"),
            P("dp", "tp"),
            P("dp", "tp"),
            P("dp", "tp"),
            P("dp", "tp"),
            P("tp", "dp"),
            P("dp"),
            P("dp", "tp"),
            P("dp", "tp"),
            P("tp", "dp"),
        ),
        check_vma=False,
    )
```
